32 devices in a mesh: fsdp: 4 (over x, core), replica: 8 (over z, y).
Axes of the slice: x: 2, y: 2, z: 4, core: 2. Of those that a mesh axis runs over, the one named last changes fastest.
Arguments:
- block_input: bfloat16 [32, 144, 960], P(('fsdp', 'replica')), may hold values from -6 to 6
- attn_gain: bfloat16 [960], P('fsdp'), may hold values from 0.25 to 1.75
- query_weight: bfloat16 [960, 960], P(None, 'fsdp'), may hold values from -0.1875 to 0.1875
- key_matrix: bfloat16 [960, 320], P(None, 'fsdp'), may hold values from -0.1875 to 0.1875
- value_matrix: bfloat16 [960, 320], P(None, 'fsdp'), may hold values from -0.1875 to 0.1875
- output_weight: bfloat16 [960, 960], P(None, 'fsdp'), may hold values from -0.375 to 0.375
- mlp_gain: bfloat16 [960], P('fsdp'), may hold values from 0.25 to 1.75
- gate_weight: bfloat16 [960, 2560], P(None, 'fsdp'), may hold values from -0.1875 to 0.1875
- up_weight: bfloat16 [960, 2560], P(None, 'fsdp'), may hold values from -0.1875 to 0.1875
- down_weight: bfloat16 [2560, 960], P(None, 'fsdp'), may hold values from -0.125 to 0.125
- segment_ids: int32 [32, 144], P(('fsdp', 'replica')), may hold values from 0 to 3, never falling along the last dimension, each value on 1 to 72 neighbouring positions
- out_grad: bfloat16 [32, 144, 960], P(('fsdp', 'replica')), may hold values from -6 to 6
Outputs:
- block_output: bfloat16 [32, 144, 960], P(('fsdp', 'replica'))
- input_grad: float32 [32, 144, 960], P(('fsdp', 'replica'))
- attn_gain_grad: float32 [960], P('fsdp')
- query_grad: float32 [960, 960], P('replica', 'fsdp')
- key_grad: float32 [960, 320], P('replica', 'fsdp')
- value_grad: float32 [960, 320], P('replica', 'fsdp')
- output_weight_grad: float32 [960, 960], P('replica', 'fsdp')
- mlp_gain_grad: float32 [960], P('fsdp')
- gate_grad: float32 [960, 2560], P('replica', 'fsdp')
- up_grad: float32 [960, 2560], P('replica', 'fsdp')
- down_grad: float32 [2560, 960], P('replica', 'fsdp')
The draws below stay inside these ranges and needn't reach their ends.
Inputs may be any that keep to these rules, and one draw needn't show every extreme that they name: `segment_ids`: along each sequence the numbers never fall and each document has 1 to 72 tokens.
All inputs are finite; a program needn't handle non-finite values.
Results may differ from the reference program's by a relative error of at most 0.017.
Values may be sent and summed in bfloat16 or wider, within the bound.
No kernel may reach another device: no remote copies, remote signals or barrier semaphores. Data moves between devices by JAX's collectives and lax.ppermute only.
A program may use at most 192 MiB of HBM per device.

```python
import math
import jax
import jax.numpy as jnp
import numpy as np
from jax import lax

MODEL_SIZE = 960
HQ = 15
KEY_VALUE_HEADS = 5
HEAD_DIMENSION = 64
FF = 2560
LEN = 144
SEQS = 32


def levels(rng, shape, split, low, largest):
    level = 1.0
    for position, blocks in split:
        draws = jax.random.uniform(jax.random.fold_in(jax.random.fold_in(rng, 6), position), (blocks,), jnp.float32, low / len(split), largest / len(split))
        level = level * jnp.repeat(jnp.exp(draws), shape[position] // blocks).reshape((-1,) + (1,) * (len(shape) - 1 - position))
    return level


def split_up(amount, total, bound, lean):
    weights = [(1 << 20) // math.isqrt(rank ** lean) + 1 for rank in range(2, amount + 1)]
    surplus, counts = total - bound - (amount - 1), [1] * (amount - 1)
    while surplus > 0:
        candidates = [i for i in range(amount - 1) if counts[i] < bound]
        pool, budget = sum([weights[i] for i in candidates]), surplus
        for i in candidates:
            addition = min(bound - counts[i], max(1, budget * weights[i] // pool), surplus)
            counts[i] = counts[i] + addition
            surplus = surplus - addition
    return np.array([bound] + counts)


def ragged(rng, count, total, bound, skew):
    if count == 2:
        one = jax.random.randint(rng, (), max(1, total - bound), min(bound, total - 1) + 1)
        return jnp.stack([one, total - one])
    sizes = jnp.asarray(split_up(count, total, bound, skew), jnp.int32)
    twos = (count - 1) // 2
    donor, sink = sizes[1:1 + 2 * twos:2], sizes[2:2 + 2 * twos:2]
    margin = jnp.minimum(donor - 1, bound - sink)
    passed = jax.random.randint(jax.random.fold_in(rng, 1), (twos,), 0, 1 << 20) % (margin + 1)
    sizes = sizes.at[1:1 + 2 * twos:2].set(donor - passed).at[2:2 + 2 * twos:2].set(sink + passed)
    return sizes[jax.random.permutation(jax.random.fold_in(rng, 2), count)]


def scatter_about(own_key, extent, deviation, most, split=(), kind=jnp.bfloat16):
    values = deviation * jax.random.normal(own_key, extent, jnp.float32)
    if split:
        values = values * levels(own_key, extent, split, -0.22, 0.18)
    return jnp.clip(values, -most, most).astype(kind)


def setup_inputs(seed: int = 0) -> dict:
    seeds = jax.random.split(jax.random.key(seed), 13)
    block_input = scatter_about(seeds[0], (SEQS, LEN, MODEL_SIZE), 1.0, 6.0, ((0, 32),))
    attn_gain = jnp.clip(1.0 + 0.15 * jax.random.normal(seeds[1], (MODEL_SIZE,), jnp.float32), 0.25, 1.75).astype(jnp.bfloat16)
    query_weight = scatter_about(seeds[2], (MODEL_SIZE, HQ * HEAD_DIMENSION), MODEL_SIZE ** -0.5, 0.1875, ((1, 4),))
    key_matrix = scatter_about(seeds[3], (MODEL_SIZE, KEY_VALUE_HEADS * HEAD_DIMENSION), MODEL_SIZE ** -0.5, 0.1875, ((1, 4),))
    value_matrix = scatter_about(seeds[4], (MODEL_SIZE, KEY_VALUE_HEADS * HEAD_DIMENSION), MODEL_SIZE ** -0.5, 0.1875, ((1, 4),))
    output_weight = scatter_about(seeds[5], (HQ * HEAD_DIMENSION, MODEL_SIZE), (HQ * HEAD_DIMENSION // 4) ** -0.5, 0.375, ((1, 4),))
    mlp_gain = jnp.clip(1.0 + 0.15 * jax.random.normal(seeds[6], (MODEL_SIZE,), jnp.float32), 0.25, 1.75).astype(jnp.bfloat16)
    gate_weight = scatter_about(seeds[7], (MODEL_SIZE, FF), MODEL_SIZE ** -0.5, 0.1875, ((1, 4),))
    up_weight = scatter_about(seeds[8], (MODEL_SIZE, FF), MODEL_SIZE ** -0.5, 0.1875, ((1, 4),))
    down_weight = scatter_about(seeds[9], (FF, MODEL_SIZE), FF ** -0.5, 0.125, ((1, 4),))
    segment_ids = jax.vmap(lambda own: jnp.searchsorted(jnp.cumsum(ragged(own, 4, LEN, LEN // 2, 0)), jnp.arange(LEN), side="right"))(jax.random.split(seeds[10], SEQS)).reshape((SEQS, LEN)).astype(jnp.int32)
    out_grad = scatter_about(seeds[11], (SEQS, LEN, MODEL_SIZE), 1.0, 6.0, ((0, 32),))
    return {"block_input": block_input, "attn_gain": attn_gain, "query_weight": query_weight, "key_matrix": key_matrix, "value_matrix": value_matrix, "output_weight": output_weight, "mlp_gain": mlp_gain, "gate_weight": gate_weight, "up_weight": up_weight, "down_weight": down_weight, "segment_ids": segment_ids, "out_grad": out_grad}


EPSILON = 1e-05
ROPE_BASE = 100000.0

def rms_forward(values, scale_gain):
    inverse = lax.rsqrt(lax.optimization_barrier(jnp.mean(values * values, -1, keepdims=True)) + EPSILON)
    normed = values * inverse
    return (normed, inverse, (normed * scale_gain.astype(jnp.float32)).astype(jnp.bfloat16))

def rms_backward(gradient, normed, inverse, scale_gain):
    scaled = gradient * scale_gain.astype(jnp.float32)
    gain_gradient = lax.optimization_barrier(jnp.sum(gradient * normed, 0))
    back = inverse * (scaled - normed * lax.optimization_barrier(jnp.mean(scaled * normed, -1, keepdims=True)))
    return (back, gain_gradient)

def rotary_tables(segment_ids):
    length = segment_ids.shape[1]
    same_doc = segment_ids[:, :, None] == segment_ids[:, None, :]
    row_index = jnp.arange(length)[:, None]
    col_index = jnp.arange(length)[None, :]
    earlier = lax.optimization_barrier(jnp.sum((same_doc & (row_index > col_index)).astype(jnp.float32), -1))
    allowed = same_doc & (row_index >= col_index)
    half_size = HEAD_DIMENSION // 2
    frequency = ROPE_BASE ** (-2.0 * jnp.arange(half_size, dtype=jnp.float32) / HEAD_DIMENSION)
    rotary_angles = earlier[:, :, None, None] * frequency
    return (jnp.cos(rotary_angles), jnp.sin(rotary_angles), allowed)

def rotate(values, cosine_table, sine_table):
    half_size = values.shape[-1] // 2
    leading_half = values[..., :half_size]
    second_half = values[..., half_size:]
    return jnp.concatenate([leading_half * cosine_table - second_half * sine_table, second_half * cosine_table + leading_half * sine_table], -1)

def rotate_back(values, cosine_table, sine_table):
    half_size = values.shape[-1] // 2
    leading_half = values[..., :half_size]
    second_half = values[..., half_size:]
    return jnp.concatenate([leading_half * cosine_table + second_half * sine_table, second_half * cosine_table - leading_half * sine_table], -1)

def round_keep(values):
    return lax.optimization_barrier(values.astype(jnp.bfloat16)).astype(jnp.float32)

def attention_scores(query_b, key_b, allowed):
    batch_size, length, head_count, head_size = query_b.shape
    group_count = key_b.shape[2]
    grouped = query_b.astype(jnp.float32).reshape(batch_size, length, group_count, head_count // group_count, head_size)
    scores = jnp.einsum('blgrd,bmgd->bgrlm', grouped, key_b.astype(jnp.float32)) * (1.0 / math.sqrt(head_size))
    return jnp.where(allowed[:, None, None], scores, -1e+30)

def forward(block_input, segment_ids, weights):
    attn_gain, query_weight, key_matrix, value_matrix, output_weight, mlp_gain, gate_weight, up_weight, down_weight = weights
    batch_size, length, model_width = block_input.shape
    head_count = query_weight.shape[1] // HEAD_DIMENSION
    group_count = key_matrix.shape[1] // HEAD_DIMENSION
    residual = block_input.reshape(-1, model_width).astype(jnp.float32)
    normed_one, inverse_one, attn_in = rms_forward(residual, attn_gain)
    cosine_table, sine_table, allowed = rotary_tables(segment_ids)
    query = jnp.dot(attn_in, query_weight, preferred_element_type=jnp.float32).reshape(batch_size, length, head_count, HEAD_DIMENSION)
    key_proj = jnp.dot(attn_in, key_matrix, preferred_element_type=jnp.float32).reshape(batch_size, length, group_count, HEAD_DIMENSION)
    query_b = rotate(query, cosine_table, sine_table).astype(jnp.bfloat16)
    key_b = rotate(key_proj, cosine_table, sine_table).astype(jnp.bfloat16)
    value_b = jnp.dot(attn_in, value_matrix, preferred_element_type=jnp.float32).astype(jnp.bfloat16).reshape(batch_size, length, group_count, HEAD_DIMENSION)
    scores = attention_scores(query_b, key_b, allowed)
    row_top = lax.optimization_barrier(jnp.max(scores, -1, keepdims=True))
    log_total = row_top + jnp.log(lax.optimization_barrier(jnp.sum(jnp.exp(scores - row_top), -1, keepdims=True)))
    probabilities = round_keep(jnp.exp(scores - log_total))
    attended = jnp.einsum('bgrlm,bmgd->blgrd', probabilities, value_b.astype(jnp.float32))
    attended = attended.astype(jnp.bfloat16).reshape(batch_size * length, head_count * HEAD_DIMENSION)
    hidden = residual + jnp.dot(attended, output_weight, preferred_element_type=jnp.float32)
    normed_two, inverse_two, mlp_in = rms_forward(hidden, mlp_gain)
    gate_values = jnp.dot(mlp_in, gate_weight, preferred_element_type=jnp.float32)
    up_values = jnp.dot(mlp_in, up_weight, preferred_element_type=jnp.float32)
    mixed_hidden = (jax.nn.silu(gate_values) * up_values).astype(jnp.bfloat16)
    result = hidden + jnp.dot(mixed_hidden, down_weight, preferred_element_type=jnp.float32)
    result = result.astype(jnp.bfloat16).reshape(batch_size, length, model_width)
    saved_state = (normed_one, inverse_one, attn_in, cosine_table, sine_table, allowed, query_b, key_b, value_b, log_total, attended, normed_two, inverse_two, mlp_in, gate_values, up_values, mixed_hidden)
    return (result, saved_state)

def backward(saved_state, out_grad, weights):
    attn_gain, query_weight, key_matrix, value_matrix, output_weight, mlp_gain, gate_weight, up_weight, down_weight = weights
    normed_one, inverse_one, attn_in, cosine_table, sine_table, allowed, query_b, key_b, value_b, log_total, attended, normed_two, inverse_two, mlp_in, gate_values, up_values, mixed_hidden = saved_state
    batch_size, length, model_width = out_grad.shape
    head_count = query_weight.shape[1] // HEAD_DIMENSION
    group_count = key_matrix.shape[1] // HEAD_DIMENSION
    group_ratio = head_count // group_count
    flat_grad = out_grad.reshape(-1, model_width)
    down_gradient = jnp.dot(mixed_hidden.T, flat_grad, preferred_element_type=jnp.float32)
    mixed_grad = jnp.dot(flat_grad, down_weight.T, preferred_element_type=jnp.float32)
    sigmoid_gate = jax.nn.sigmoid(gate_values)
    swish_gate = gate_values * sigmoid_gate
    gate_back = (mixed_grad * up_values * sigmoid_gate * (1.0 + gate_values * (1.0 - sigmoid_gate))).astype(jnp.bfloat16)
    up_back = (mixed_grad * swish_gate).astype(jnp.bfloat16)
    gate_gradient = jnp.dot(mlp_in.T, gate_back, preferred_element_type=jnp.float32)
    up_gradient = jnp.dot(mlp_in.T, up_back, preferred_element_type=jnp.float32)
    mlp_in_grad = jnp.dot(gate_back, gate_weight.T, preferred_element_type=jnp.float32) + jnp.dot(up_back, up_weight.T, preferred_element_type=jnp.float32)
    hidden_norm_grad, mlp_gain_gradient = rms_backward(mlp_in_grad, normed_two, inverse_two, mlp_gain)
    hidden_grad = flat_grad.astype(jnp.float32) + hidden_norm_grad
    hidden_back = hidden_grad.astype(jnp.bfloat16)
    output_gradient = jnp.dot(attended.T, hidden_back, preferred_element_type=jnp.float32)
    attended_grad = jnp.dot(hidden_back, output_weight.T, preferred_element_type=jnp.float32).astype(jnp.bfloat16)
    grouped_grad = attended_grad.astype(jnp.float32).reshape(batch_size, length, group_count, group_ratio, HEAD_DIMENSION)
    scores = attention_scores(query_b, key_b, allowed)
    soft_weights = jnp.exp(scores - log_total)
    probabilities = round_keep(soft_weights)
    value_back = jnp.einsum('bgrlm,blgrd->bmgd', probabilities, grouped_grad).astype(jnp.bfloat16)
    prob_grad = jnp.einsum('blgrd,bmgd->bgrlm', grouped_grad, value_b.astype(jnp.float32))
    row_delta = lax.optimization_barrier(jnp.sum(grouped_grad * attended.astype(jnp.float32).reshape(batch_size, length, group_count, group_ratio, HEAD_DIMENSION), -1))
    row_delta = jnp.transpose(row_delta, (0, 2, 3, 1))[..., None]
    score_grad = round_keep(soft_weights * (prob_grad - row_delta) * (1.0 / math.sqrt(HEAD_DIMENSION)))
    query_back = jnp.einsum('bgrlm,bmgd->blgrd', score_grad, key_b.astype(jnp.float32)).reshape(batch_size, length, head_count, HEAD_DIMENSION)
    query_back = rotate_back(query_back, cosine_table, sine_table).astype(jnp.bfloat16).reshape(-1, head_count * HEAD_DIMENSION)
    grouped_query = query_b.astype(jnp.float32).reshape(batch_size, length, group_count, group_ratio, HEAD_DIMENSION)
    key_back = jnp.einsum('bgrlm,blgrd->bmgd', score_grad, grouped_query)
    key_back = rotate_back(key_back, cosine_table, sine_table).astype(jnp.bfloat16).reshape(-1, group_count * HEAD_DIMENSION)
    value_back = value_back.reshape(-1, group_count * HEAD_DIMENSION)
    query_gradient = jnp.dot(attn_in.T, query_back, preferred_element_type=jnp.float32)
    key_gradient = jnp.dot(attn_in.T, key_back, preferred_element_type=jnp.float32)
    value_gradient = jnp.dot(attn_in.T, value_back, preferred_element_type=jnp.float32)
    attn_in_grad = jnp.dot(query_back, query_weight.T, preferred_element_type=jnp.float32)
    attn_in_grad = attn_in_grad + jnp.dot(key_back, key_matrix.T, preferred_element_type=jnp.float32)
    attn_in_grad = attn_in_grad + jnp.dot(value_back, value_matrix.T, preferred_element_type=jnp.float32)
    input_norm_grad, attn_gain_gradient = rms_backward(attn_in_grad, normed_one, inverse_one, attn_gain)
    input_gradient = (hidden_grad + input_norm_grad).reshape(batch_size, length, model_width)
    return (input_gradient, (attn_gain_gradient, query_gradient, key_gradient, value_gradient, output_gradient, mlp_gain_gradient, gate_gradient, up_gradient, down_gradient))

def reference(block_input, attn_gain, query_weight, key_matrix, value_matrix, output_weight, mlp_gain, gate_weight, up_weight, down_weight, segment_ids, out_grad):
    weights = (attn_gain, query_weight, key_matrix, value_matrix, output_weight, mlp_gain, gate_weight, up_weight, down_weight)

    def one_sequence(totals, sequence_items):
        tokens, segments, cotangent = sequence_items
        result, saved_state = forward(tokens[None], segments[None], weights)
        input_gradient, gradients = backward(saved_state, cotangent[None], weights)
        totals = tuple((left + right for left, right in zip(totals, gradients)))
        return (totals, (result[0], input_gradient[0]))
    initial = tuple((jnp.zeros(weight.shape, jnp.float32) for weight in weights))
    totals, (outputs, input_grads) = lax.scan(one_sequence, initial, (block_input, segment_ids, out_grad))
    return (outputs, input_grads, totals[0], totals[1], totals[2], totals[3], totals[4], totals[5], totals[6], totals[7], totals[8])
```

```python
import math

import jax
import jax.numpy as jnp
from jax import lax
from jax.sharding import PartitionSpec as P

HEAD_DIMENSION = 64
EPSILON = 1e-05
ROPE_BASE = 100000.0
BF = jnp.bfloat16
F32 = jnp.float32


def dot(left, right):
    return jnp.dot(left, right, preferred_element_type=F32)


def rows_product(left, right):
    return lax.dot_general(left, right, (((0,), (0,)), ((), ())), preferred_element_type=F32)


def back_product(left, weight):
    return lax.dot_general(left, weight, (((1,), (1,)), ((), ())), preferred_element_type=F32)


def swap_fsdp(value, bit):
    return lax.ppermute(value, "fsdp", [(i, i ^ bit) for i in range(4)])


def swap_replica(value, bit, count):
    return lax.ppermute(value, "replica", [(i, i ^ bit) for i in range(count)])


def reorder(blocks, me):
    b = [blocks[i] for i in range(4)]
    core = (me & 1) == 1
    across = (me & 2) == 2
    s = [
        jnp.where(core, b[1], b[0]),
        jnp.where(core, b[0], b[1]),
        jnp.where(core, b[3], b[2]),
        jnp.where(core, b[2], b[3]),
    ]
    return [
        jnp.where(across, s[2], s[0]),
        jnp.where(across, s[3], s[1]),
        jnp.where(across, s[0], s[2]),
        jnp.where(across, s[1], s[3]),
    ]


def gather_group(value):
    far = swap_fsdp(value, 2)
    pair = swap_fsdp(jnp.stack([value, far]), 1)
    return [value, pair[0], far, pair[1]]


def exchange_group(blocks):
    far = swap_fsdp(jnp.stack([blocks[2], blocks[3]]), 2)
    near = swap_fsdp(jnp.stack([blocks[1], far[1]]), 1)
    return [blocks[0], near[0], far[0], near[1]]


def scatter_group(parts):
    near = swap_fsdp(jnp.stack([parts[1], parts[3]]).astype(BF), 1)
    own = parts[0].astype(F32) + near[0].astype(F32)
    other = (parts[2].astype(F32) + near[1].astype(F32)).astype(BF)
    return own + swap_fsdp(other, 2).astype(F32)


def scatter_replica(block, order, count):
    bits = count.bit_length() - 1
    rows, width = block.shape
    me = lax.axis_index("replica")
    value = block.reshape((2,) * bits + (rows // count, width))
    axes = list(range(bits - 1, -1, -1))
    for step, bit in enumerate(order):
        axis = axes.index(bit)
        mine = (me >> bit) & 1
        keep = lax.dynamic_index_in_dim(value, mine, axis, keepdims=False)
        send = lax.dynamic_index_in_dim(value, 1 - mine, axis, keepdims=False)
        total = keep.astype(F32) + swap_replica(send.astype(BF), 1 << bit, count).astype(F32)
        value = total if step == bits - 1 else total.astype(BF)
        axes.pop(axis)
    return value


def rms_forward(values, scale_gain):
    inverse = lax.rsqrt(jnp.mean(values * values, -1, keepdims=True) + EPSILON)
    normed = values * inverse
    return (normed, inverse, (normed * scale_gain.astype(F32)).astype(BF))


def rms_backward(gradient, normed, inverse, scale_gain):
    scaled = gradient * scale_gain.astype(F32)
    gain_gradient = jnp.sum(gradient * normed, 0)
    back = inverse * (scaled - normed * jnp.mean(scaled * normed, -1, keepdims=True))
    return (back, gain_gradient)


def rotary_tables(segment_ids):
    length = segment_ids.shape[0]
    same_doc = segment_ids[:, None] == segment_ids[None, :]
    row_index = jnp.arange(length)[:, None]
    col_index = jnp.arange(length)[None, :]
    earlier = jnp.sum((same_doc & (row_index > col_index)).astype(F32), -1)
    allowed = same_doc & (row_index >= col_index)
    half_size = HEAD_DIMENSION // 2
    frequency = ROPE_BASE ** (-2.0 * jnp.arange(half_size, dtype=F32) / HEAD_DIMENSION)
    angles = earlier[:, None, None] * frequency
    return (jnp.cos(angles), jnp.sin(angles), allowed)


def rotate(values, cosine_table, sine_table):
    half_size = values.shape[-1] // 2
    a = values[..., :half_size]
    b = values[..., half_size:]
    return jnp.concatenate([a * cosine_table - b * sine_table, b * cosine_table + a * sine_table], -1)


def local(
    replicas,
    block_input,
    attn_gain,
    query_weight,
    key_matrix,
    value_matrix,
    output_weight,
    mlp_gain,
    gate_weight,
    up_weight,
    down_weight,
    segment_ids,
    out_grad,
):
    me = lax.axis_index("fsdp")
    length, width = block_input.shape[1:]
    qw, kw = query_weight.shape[1], key_matrix.shape[1]
    heads, groups = 4 * qw // HEAD_DIMENSION, 4 * kw // HEAD_DIMENSION
    ratio = heads // groups
    hidden_units = gate_weight.shape[1]
    og = out_grad[0]

    proj = jnp.concatenate([query_weight, key_matrix, value_matrix], 1)
    proj_all = gather_group(proj)
    gains = jnp.stack([attn_gain, mlp_gain])
    gains_all = jnp.concatenate(reorder(gather_group(gains), me), 1)
    attn_gain_all, mlp_gain_all = gains_all[0], gains_all[1]
    out_all = gather_group(output_weight)
    og_all = jnp.concatenate(gather_group(og), 0)
    down_blocks = reorder(down_weight.reshape(4, hidden_units, qw), me)
    down_rows = jnp.concatenate(reorder(exchange_group(down_blocks), me), 1)

    residual = block_input[0].astype(F32)
    normed_one, inverse_one, n1 = rms_forward(residual, attn_gain_all)
    cosine, sine, allowed = rotary_tables(segment_ids[0])
    qkv = reorder([dot(n1, w) for w in proj_all], me)
    query = jnp.concatenate([b[:, :qw] for b in qkv], 1).reshape(length, heads, HEAD_DIMENSION)
    key = jnp.concatenate([b[:, qw : qw + kw] for b in qkv], 1).reshape(length, groups, HEAD_DIMENSION)
    value_b = (
        jnp.concatenate([b[:, qw + kw :] for b in qkv], 1).astype(BF).reshape(length, groups, HEAD_DIMENSION)
    )
    query_b = rotate(query, cosine, sine).astype(BF).reshape(length, groups, ratio, HEAD_DIMENSION)
    key_b = rotate(key, cosine, sine).astype(BF)
    scale = 1.0 / math.sqrt(HEAD_DIMENSION)
    scores = jnp.einsum("lgrd,mgd->grlm", query_b, key_b, preferred_element_type=F32) * scale
    scores = jnp.where(allowed[None, None], scores, -1e30)
    top = jnp.max(scores, -1, keepdims=True)
    raw = jnp.exp(scores - top)
    soft = raw / jnp.sum(raw, -1, keepdims=True)
    prob = soft.astype(BF)
    attended = jnp.einsum("grlm,mgd->lgrd", prob, value_b, preferred_element_type=F32)
    attended = attended.astype(BF).reshape(length, heads * HEAD_DIMENSION)
    hidden = residual + jnp.concatenate(reorder([dot(attended, w) for w in out_all], me), 1)
    normed_two, inverse_two, n2 = rms_forward(hidden, mlp_gain_all)

    n2_all = jnp.concatenate(gather_group(n2), 0)
    side = [jnp.concatenate(p, 0) for p in (zip(*[(g[0], g[1]) for g in gather_group(jnp.stack([n1, attended]))]))]
    n1_all, attended_all = side
    gate = dot(n2_all, gate_weight)
    up = dot(n2_all, up_weight)
    dm = back_product(og_all, down_rows)
    sig = jax.nn.sigmoid(gate)
    swish = gate * sig
    mixed = (swish * up).astype(BF)
    dg = (dm * up * sig * (1.0 + gate * (1.0 - sig))).astype(BF)
    du = (dm * swish).astype(BF)
    dn2_part = back_product(dg, gate_weight) + back_product(du, up_weight)
    dn2 = scatter_group(dn2_part.reshape(4, length, width))
    bo_part = dot(mixed, down_rows)
    bo = scatter_group(bo_part.reshape(4, length, width))
    result = (hidden + bo).astype(BF)[None]
    gate_grad = rows_product(n2_all, dg).astype(BF)
    up_grad = rows_product(n2_all, du).astype(BF)
    down_part = rows_product(mixed, og_all).astype(BF)
    down_cols = reorder([down_part[:, j * qw : (j + 1) * qw] for j in range(4)], me)
    down_grad = jnp.concatenate(reorder(exchange_group(down_cols), me), 0)

    bits = replicas.bit_length() - 1
    first = [0] + list(range(1, bits))
    second = list(range(1, bits))
    second.insert(1, 0)
    gate_total = scatter_replica(gate_grad, first, replicas)
    up_total = scatter_replica(up_grad, second, replicas)
    down_total = scatter_replica(down_grad, first, replicas)

    back, mlp_gain_part = rms_backward(dn2, normed_two, inverse_two, mlp_gain_all)
    dhidden = og.astype(F32) + back
    db = dhidden.astype(BF)
    db_blocks = reorder([db[:, j * qw : (j + 1) * qw] for j in range(4)], me)
    db_all = jnp.concatenate(exchange_group(db_blocks), 0)
    out_total = scatter_replica(rows_product(attended_all, db_all).astype(BF), second, replicas)
    do = sum(back_product(db_blocks[k], out_all[k]) for k in range(4)).astype(BF)
    do = do.reshape(length, groups, ratio, HEAD_DIMENSION)
    dv = jnp.einsum("grlm,lgrd->mgd", prob, do, preferred_element_type=F32).astype(BF)
    dp = jnp.einsum("lgrd,mgd->grlm", do, value_b, preferred_element_type=F32)
    delta = jnp.sum(do.astype(F32) * attended.astype(F32).reshape(do.shape), -1)
    delta = jnp.transpose(delta, (1, 2, 0))[..., None]
    ds = (soft * (dp - delta) * scale).astype(BF)
    dq = jnp.einsum("grlm,mgd->lgrd", ds, key_b, preferred_element_type=F32).reshape(length, heads, HEAD_DIMENSION)
    dk = jnp.einsum("grlm,lgrd->mgd", ds, query_b, preferred_element_type=F32)
    dq = rotate(dq, cosine, -sine).astype(BF).reshape(length, -1)
    dk = rotate(dk, cosine, -sine).astype(BF).reshape(length, -1)
    dv = dv.reshape(length, -1)
    dqkv = [
        jnp.concatenate(
            [dq[:, j * qw : (j + 1) * qw], dk[:, j * kw : (j + 1) * kw], dv[:, j * kw : (j + 1) * kw]], 1
        )
        for j in range(4)
    ]
    dqkv = reorder(dqkv, me)
    dqkv_all = jnp.concatenate(exchange_group(dqkv), 0)
    dn1 = sum(back_product(dqkv[k], proj_all[k]) for k in range(4))
    back_one, attn_gain_part = rms_backward(dn1, normed_one, inverse_one, attn_gain_all)
    input_grad = (dhidden + back_one)[None]
    qkv_total = scatter_replica(rows_product(n1_all, dqkv_all).astype(BF), first, replicas)

    total = jnp.stack([attn_gain_part, mlp_gain_part])
    for bit in range(2):
        total = total + swap_fsdp(total, 1 << bit)
    for bit in range(bits):
        total = total + swap_replica(total, 1 << bit, replicas)
    total = lax.dynamic_slice_in_dim(total, me * qw, qw, 1)
    return (
        result,
        input_grad,
        total[0],
        qkv_total[:, :qw],
        qkv_total[:, qw : qw + kw],
        qkv_total[:, qw + kw :],
        out_total,
        total[1],
        gate_total,
        up_total,
        down_total,
    )


def solution(mesh):
    replicas = mesh.shape["replica"]

    def body(*args):
        return local(replicas, *args)

    rows = P(("fsdp", "replica"), None, None)
    cols = P(None, "fsdp")
    both = P("replica", "fsdp")
    return jax.shard_map(
        body,
        mesh=mesh,
        in_specs=(
            rows, P("fsdp"), cols, cols, cols, cols, P("fsdp"), cols, cols, cols,
            P(("fsdp", "replica"), None), rows,
        ),
        out_specs=(rows, rows, P("fsdp"), both, both, both, both, P("fsdp"), both, both, both),
        check_vma=False,
    )
```

```python
import functools
import math

import jax
import jax.numpy as jnp
from jax import lax
from jax.experimental import pallas as pl
from jax.experimental.pallas import tpu as pltpu
from jax.sharding import PartitionSpec as P


HEAD_DIMENSION = 64
EPSILON = 1e-05
ROPE_BASE = 100000.0
BF = jnp.bfloat16
F32 = jnp.float32


def dot(left, right):
    return jnp.dot(left, right, preferred_element_type=F32)


def rows_product(left, right):
    return lax.dot_general(left, right, (((0,), (0,)), ((), ())), preferred_element_type=F32)


def back_product(left, weight):
    return lax.dot_general(left, weight, (((1,), (1,)), ((), ())), preferred_element_type=F32)


def swap_fsdp(value, bit):
    return lax.ppermute(value, "fsdp", [(i, i ^ bit) for i in range(4)])


def swap_replica(value, bit, count):
    return lax.ppermute(value, "replica", [(i, i ^ bit) for i in range(count)])


def gather_group(value):
    far = swap_fsdp(value, 2)
    near = swap_fsdp(value, 1)
    return [value, near, far, swap_fsdp(far, 1)]


def gather_halves(value, half, replicas):
    far_a = swap_fsdp(half, 2)
    near = swap_fsdp(value, 1)
    far_b = swap_replica(far_a, 1, replicas)
    return [
        value, near, far_a, far_b,
        swap_fsdp(far_a, 1), swap_fsdp(far_b, 1),
    ]


def exchange_parts(own, near, far):
    came = swap_fsdp(far, 2)
    return [own, swap_fsdp(near, 1), came[0], swap_fsdp(came[1], 1)]


def exchange_four(own, near, far, diagonal):
    came = swap_fsdp(far, 2)
    passed = swap_fsdp(diagonal, 2)
    return [own, swap_fsdp(near, 1), came, swap_fsdp(passed, 1)]


def scatter_parts(own, far, near):
    came = swap_fsdp(near, 1).astype(F32)
    other = swap_fsdp((far + came[1]).astype(BF), 2)
    return own + came[0], other


def scatter_replica(pair, order, replicas, widths, turned):
    keep, send = pair
    left = sorted(order)
    for step, bit in enumerate(order):
        left.remove(bit)
        came = swap_replica(send, 1 << bit, replicas)
        if left:
            keep, send = fold(keep, came, left, order[step + 1])
        else:
            return fold_last(keep, came, widths, turned)


def rotary_tables(earlier):
    lanes = lax.broadcasted_iota(jnp.int32, (1, 128), 1)
    half_size = HEAD_DIMENSION // 2
    index = (lanes % half_size).astype(F32)
    frequency = jnp.exp(index * (-2.0 * math.log(ROPE_BASE) / HEAD_DIMENSION))
    angles = earlier * frequency
    sine = jnp.sin(angles)
    return jnp.cos(angles), jnp.where(lanes % HEAD_DIMENSION < half_size, -sine, sine)


SPARE = 3 << 20
VMEM_SPEC = pl.BlockSpec(memory_space=pltpu.VMEM)
HBM_SPEC = pl.BlockSpec(memory_space=pltpu.HBM)


def call(kernel, out_shape, args, spaces, scratch, flops=0):
    bytes_accessed = sum(a.size * a.dtype.itemsize for a in list(args) + jax.tree.leaves(out_shape))
    size = lambda a: math.prod(a.shape[:-1]) * pad_lanes(a.shape[-1]) * jnp.dtype(a.dtype).itemsize
    held = [a for a, c in zip(args, spaces) if c == "v"] + jax.tree.leaves(out_shape)
    held += [a for a in scratch if isinstance(a, type(pltpu.VMEM((8, 128), F32))) and len(a.shape) > 1]
    room = sum(size(a) for a in held) + SPARE
    args = [pltpu.with_memory_space_constraint(a, pltpu.HBM) if c == "h" else a for a, c in zip(args, spaces)]
    return pl.pallas_call(
        kernel,
        out_shape=out_shape,
        in_specs=[VMEM_SPEC if c == "v" else HBM_SPEC for c in spaces],
        out_specs=jax.tree.map(lambda _: VMEM_SPEC, out_shape),
        scratch_shapes=scratch,
        cost_estimate=pl.CostEstimate(flops=flops, transcendentals=0, bytes_accessed=bytes_accessed),
        compiler_params=pltpu.CompilerParams(vmem_limit_bytes=room),
    )(*args)


def start_all(pairs, sems, base=0):
    copies = [pltpu.make_async_copy(a, b, sems.at[base + i]) for i, (a, b) in enumerate(pairs)]
    for copy in copies:
        copy.start()
    return copies


def wait_all(copies):
    for copy in copies:
        copy.wait()


def half_places(rows):
    parity = jnp.bitwise_and(lax.axis_index("replica"), 1)
    half = half_rows(rows)
    rest = rows - half
    start_a = pl.multiple_of(parity * rest, 16)
    skip = pl.multiple_of((1 - parity) * (half - rest), 16)
    start_b = pl.multiple_of((1 - parity) * half, 16)
    return pl.ds(start_a, half), pl.ds(skip, rest), pl.ds(start_b, rest)


def fetch_blocks(sources, target, sems, base=0):
    me = lax.axis_index("fsdp")
    own, near, far_a, far_b, diag_a, diag_b = sources
    a_at, b_from, b_at = half_places(own.shape[0])
    block = [target.at[jnp.bitwise_xor(me, k)] for k in range(4)]
    pairs = [(own, block[0]), (near, block[1])]
    for k, a, b in ((2, far_a, far_b), (3, diag_a, diag_b)):
        pairs += [(a, block[k].at[a_at]), (b.at[b_from], block[k].at[b_at])]
    return start_all(pairs, sems, base)


def half_rows(rows):
    return -(-rows // 32) * 16


def fetch_down(sources, target, sems):
    me = lax.axis_index("fsdp")
    own, near, far_a, far_b, diag_a, diag_b = sources
    rows, units = near.shape
    a_at, b_from, b_at = half_places(rows)
    core = pl.multiple_of(jnp.bitwise_and(me, 1) * units, units)
    block = [target.at[pl.ds(pl.multiple_of(jnp.bitwise_xor(me, k) * rows, rows), rows)] for k in range(4)]
    return start_all(
        [
            (own.at[:, pl.ds(pl.multiple_of(me * units, units), units)], block[0]),
            (near, block[1]),
            (far_a.at[:, pl.ds(core, units)], block[2].at[a_at]),
            (far_b.at[b_from, pl.ds(core, units)], block[2].at[b_at]),
            (diag_a.at[:, pl.ds(core, units)], block[3].at[a_at]),
            (diag_b.at[b_from, pl.ds(core, units)], block[3].at[b_at]),
        ],
        sems,
    )


def swap_halves(values):
    lanes = values.shape[1]
    half = HEAD_DIMENSION // 2
    index = lax.broadcasted_iota(jnp.int32, values.shape, 1)
    return jnp.where(
        index % HEAD_DIMENSION < half, pltpu.roll(values, lanes - half, 1), pltpu.roll(values, half, 1)
    )


def widen(table, lanes):
    return jnp.concatenate([table] * (lanes // table.shape[1]), 1)


def allowed_pairs(segments):
    length = segments.shape[1]
    row = lax.broadcasted_iota(jnp.int32, (length, length), 0)
    col = lax.broadcasted_iota(jnp.int32, (length, length), 1)
    keys = jnp.broadcast_to(segments.astype(F32), (length, length))
    return jnp.where((keys == keys.T) & (row >= col), 1.0, 0.0)


def heads_of(ref, group, ratio, base=0):
    d = HEAD_DIMENSION
    starts = [base + (group * ratio + r) * d for r in range(ratio)]
    return jnp.concatenate([ref[:, a : a + d] for a in starts], 0)


def probabilities(queries, keys, mask):
    scores = back_product(queries, keys) * (1.0 / math.sqrt(HEAD_DIMENSION))
    scores = jnp.where(mask, scores, -1e30)
    top = jnp.max(scores, -1, keepdims=True)
    total = top + jnp.log(jnp.sum(jnp.exp(scores - top), -1, keepdims=True))
    return jnp.exp(scores - total)


def half_start(rows):
    parity = jnp.bitwise_and(lax.axis_index("replica"), 1)
    return pl.multiple_of(parity * (rows - half_rows(rows)), 16)


def pack_kernel(
    q_ref, ow_ref, dw_ref, k_ref, v_ref, ga_ref, gm_ref, kv_ref, q_half, kv_half, ow_half, dw_half, dw_near,
    ga_s, gm_s, sems,
):
    me = lax.axis_index("fsdp")
    units = dw_near.shape[1]
    rows_of = lambda full, half: pl.ds(half_start(full.shape[0]), half.shape[0])
    across = pl.multiple_of((1 - lax.shift_right_logical(me, 1)) * 2 * units, 128)
    mate = pl.multiple_of(jnp.bitwise_xor(me, 1) * units, 128)
    kw = k_ref.shape[0]
    qw = ga_ref.shape[0]
    small = [
        (k_ref, kv_ref.at[pl.ds(0, kw)]),
        (v_ref, kv_ref.at[pl.ds(kw, kw)]),
        (ga_ref, ga_s),
        (gm_ref, gm_s),
    ]
    large = [
        (q_ref.at[rows_of(q_ref, q_half)], q_half),
        (ow_ref.at[rows_of(ow_ref, ow_half)], ow_half),
        (dw_ref.at[rows_of(dw_ref, dw_half), pl.ds(across, 2 * units)], dw_half),
        (dw_ref.at[:, pl.ds(mate, units)], dw_near),
    ]
    small, large = start_all(small, sems), start_all(large, sems, len(small))
    wait_all(small)
    row = lax.broadcasted_iota(jnp.int32, (16, qw), 0)
    first, second = (jnp.broadcast_to(r[...].astype(F32)[None, :], (16, qw)) for r in (ga_s, gm_s))
    kv_ref[2 * kw :, :] = jnp.zeros((16, kv_ref.shape[1]), BF)
    kv_ref[2 * kw :, :qw] = jnp.where(row == 0, first, second).astype(BF)
    half = kv_half.shape[0]
    parity = jnp.bitwise_and(lax.axis_index("replica"), 1)

    @pl.when(parity == 0)
    def _():
        kv_half[...] = kv_ref[:half, :]

    @pl.when(parity == 1)
    def _():
        kv_half[...] = kv_ref[kv_ref.shape[0] - half :, :]

    wait_all(large)


def pack(query_weight, output_weight, turned, keys, values, attn_gain, mlp_gain):
    width, qw = query_weight.shape
    kw = keys.shape[0]
    units = turned.shape[1] // 4
    f = lambda *shape: jax.ShapeDtypeStruct(shape, BF)
    return call(
        pack_kernel,
        (
            f(2 * kw + 16, width), f(half_rows(width), qw), f(half_rows(2 * kw + 16), width),
            f(half_rows(output_weight.shape[0]), qw), f(half_rows(qw), 2 * units), f(qw, units),
        ),
        (query_weight, output_weight, turned, keys, values, attn_gain, mlp_gain),
        "h" * 7,
        [pltpu.VMEM((qw,), BF), pltpu.VMEM((qw,), BF), pltpu.SemaphoreType.DMA((8,))],
    )


def attention_kernel(qw, kw, *refs):
    x_ref, segments_ref = refs[:2]
    both_ref, q_ref, k_ref, v_ref, gains_ref, cos_ref, sin_ref, allowed_ref, wq, wkv, q_s, k_s, sems = refs[14:]
    copies = fetch_blocks(refs[2:8], wq, sems) + fetch_blocks(refs[8:14], wkv, sems, 6)
    allowed = allowed_pairs(segments_ref[...])
    allowed_ref[...] = allowed
    cos_ref[...], sin_ref[...] = rotary_tables(jnp.sum(allowed, -1, keepdims=True) - 1.0)
    groups = 4 * kw // HEAD_DIMENSION
    ratio = qw // kw
    x = x_ref[...].astype(F32)
    normed = x * lax.rsqrt(jnp.mean(x * x, -1, keepdims=True) + EPSILON)
    mask = jnp.concatenate([allowed] * ratio, 0) > 0.5
    wait_all(copies)
    for j in range(4):
        gains_ref[:, j * qw : (j + 1) * qw] = wkv[j, 2 * kw : 2 * kw + 16, :qw].astype(F32)
    n1 = (normed * gains_ref[0:1, :]).astype(BF)
    width = x_ref.shape[1]
    base = both_ref.shape[1] // 2
    both_ref[:, :width] = n1
    for j in range(4):
        q_s[:, j * qw : (j + 1) * qw] = dot(n1, wq[j])
        two = back_product(n1, wkv[j, : 2 * kw, :])
        k_s[:, j * kw : (j + 1) * kw] = two[:, :kw]
        v_ref[:, j * kw : (j + 1) * kw] = two[:, kw:].astype(BF)
    for source, target in ((q_s, q_ref), (k_s, k_ref)):
        values = source[...]
        lanes = values.shape[1]
        turned = values * widen(cos_ref[...], lanes) + swap_halves(values) * widen(sin_ref[...], lanes)
        target[...] = turned[:, : target.shape[1]].astype(BF)
    length = x_ref.shape[0]
    d = HEAD_DIMENSION
    for g in range(groups):
        prob = probabilities(heads_of(q_ref, g, ratio), k_ref[:, g * d : (g + 1) * d], mask)
        out = dot(prob.astype(BF), v_ref[:, g * d : (g + 1) * d]).astype(BF)
        for r in range(ratio):
            h = g * ratio + r
            both_ref[:, base + h * d : base + (h + 1) * d] = out[r * length : (r + 1) * length]


def pad_lanes(n):
    return -(-n // 128) * 128


def attention_forward(x, segments, wq, wkv, qw, kw):
    length, width = x.shape
    f = lambda *shape: jax.ShapeDtypeStruct(shape, BF)
    return call(
        functools.partial(attention_kernel, qw, kw),
        (
            f(length, 2 * pad_lanes(width)), f(length, 4 * qw), f(length, 4 * kw), f(length, 4 * kw),
            jax.ShapeDtypeStruct((16, width), F32),
            jax.ShapeDtypeStruct((length, 128), F32),
            jax.ShapeDtypeStruct((length, 128), F32),
            jax.ShapeDtypeStruct((length, length), F32),
        ),
        (x, segments, *wq, *wkv),
        "v" * 2 + "a" * 12,
        [
            pltpu.VMEM((4,) + wq[0].shape, BF),
            pltpu.VMEM((4,) + wkv[0].shape, BF),
            pltpu.VMEM((length, pad_lanes(4 * qw)), F32),
            pltpu.VMEM((length, pad_lanes(4 * kw)), F32),
            pltpu.SemaphoreType.DMA((12,)),
        ],
        2 * length * width * 4 * (qw + 2 * kw),
    )


def hidden_kernel(*refs):
    both_ref, x_ref, gains_ref = refs[:3]
    hidden_ref, n2_ref, w_s, sems = refs[9:]
    copies = fetch_blocks(refs[3:9], w_s, sems)
    qw = w_s.shape[2]
    base = both_ref.shape[1] // 2
    attended = both_ref[:, base : base + x_ref.shape[1]]
    wait_all(copies)
    for j in range(4):
        part = slice(j * qw, (j + 1) * qw)
        hidden_ref[:, part] = x_ref[:, part].astype(F32) + dot(attended, w_s[j])
    hidden = hidden_ref[...]
    normed = hidden * lax.rsqrt(jnp.mean(hidden * hidden, -1, keepdims=True) + EPSILON)
    n2_ref[...] = (normed * gains_ref[1:2, :]).astype(BF)


def hidden_forward(both, x, gains, wo):
    return call(
        hidden_kernel,
        (jax.ShapeDtypeStruct(x.shape, F32), jax.ShapeDtypeStruct(x.shape, BF)),
        (both, x, gains, *wo),
        "v" * 3 + "a" * 6,
        [pltpu.VMEM((4,) + wo[0].shape, BF), pltpu.SemaphoreType.DMA((6,))],
        2 * x.size * x.shape[1],
    )


def backward_kernel(qw, kw, *refs):
    (dn2_a, dn2_b, hidden_ref, og_ref, gains_ref, q_ref, k_ref, v_ref, both_ref, cos_ref,
     sin_ref, allowed_ref) = refs[:12]
    (dhidden_ref, gain_ref, dx0, dx1, dx23, dqkv_ref, w_s, do_s, dq_s, dk_s, dv_s, x_s, sems) = refs[18:]
    copies = fetch_blocks(refs[12:18], w_s, sems)
    base = both_ref.shape[1] // 2
    cols = qw + 2 * kw
    me = lax.axis_index("fsdp")
    length = hidden_ref.shape[0]
    d = HEAD_DIMENSION
    groups = 4 * kw // d
    ratio = qw // kw
    dn2 = dn2_a[...] + dn2_b[...].astype(F32)
    hidden = hidden_ref[...]
    inverse = lax.rsqrt(jnp.mean(hidden * hidden, -1, keepdims=True) + EPSILON)
    normed = hidden * inverse
    gain_ref[...] = jnp.sum(dn2 * normed, 0, keepdims=True)
    scaled = dn2 * gains_ref[1:2, :]
    back = inverse * (scaled - normed * jnp.mean(scaled * normed, -1, keepdims=True))
    dhidden = og_ref[...].astype(F32) + back
    dhidden_ref[...] = dhidden
    db = dhidden.astype(BF)
    for copy in copies:
        copy.wait()
    do = None
    for j in range(4):
        part = db[:, j * qw : (j + 1) * qw]
        x_s[jnp.bitwise_xor(me, j), :, cols:] = part
        term = back_product(part, w_s[j])
        do = term if do is None else do + term
    do_s[...] = do.astype(BF)
    mask = jnp.concatenate([allowed_ref[...]] * ratio, 0) > 0.5
    for g in range(groups):
        at = slice(g * d, (g + 1) * d)
        queries = heads_of(q_ref, g, ratio)
        keys = k_ref[:, at]
        soft = probabilities(queries, keys, mask)
        grad = heads_of(do_s, g, ratio)
        dv_s[:, at] = rows_product(soft.astype(BF), grad)
        dp = back_product(grad, v_ref[:, at])
        delta = jnp.sum(grad.astype(F32) * heads_of(both_ref, g, ratio, base).astype(F32), -1, keepdims=True)
        ds = (soft * (dp - delta) * (1.0 / math.sqrt(d))).astype(BF)
        dq = dot(ds, keys)
        for r in range(ratio):
            h = g * ratio + r
            dq_s[:, h * d : (h + 1) * d] = dq[r * length : (r + 1) * length]
        dk_s[:, at] = rows_product(ds, queries)
    for ref in (dq_s, dk_s):
        values = ref[...]
        lanes = values.shape[1]
        ref[...] = values * widen(cos_ref[...], lanes) - swap_halves(values) * widen(sin_ref[...], lanes)
    dqkv_ref[:, : 4 * qw] = dq_s[:, : 4 * qw].astype(BF)
    for j in range(4):
        k_at = 4 * qw + 2 * j * kw
        dqkv_ref[:, k_at : k_at + kw] = dk_s[:, j * kw : (j + 1) * kw].astype(BF)
        dqkv_ref[:, k_at + kw : k_at + 2 * kw] = dv_s[:, j * kw : (j + 1) * kw].astype(BF)
        at = jnp.bitwise_xor(me, j)
        x_s[at, :, :qw] = dq_s[:, j * qw : (j + 1) * qw].astype(BF)
        x_s[at, :, qw : qw + kw] = dk_s[:, j * kw : (j + 1) * kw].astype(BF)
        x_s[at, :, qw + kw : cols] = dv_s[:, j * kw : (j + 1) * kw].astype(BF)
    dx0[...] = x_s[0]
    dx1[...] = x_s[1]
    dx23[...] = x_s[2:4]


def attention_backward(dn2_a, dn2_b, hidden, og, gains, q, k, v, both, cos, sin, allowed, wo, qw, kw):
    length, width = hidden.shape
    cols = 2 * qw + 2 * kw
    f = lambda *shape: jax.ShapeDtypeStruct(shape, BF)
    return call(
        functools.partial(backward_kernel, qw, kw),
        (
            jax.ShapeDtypeStruct(hidden.shape, F32),
            jax.ShapeDtypeStruct((1, width), F32),
            f(length, cols), f(length, cols), f(2, length, cols),
            f(length, 4 * (qw + 2 * kw)),
        ),
        (dn2_a, dn2_b, hidden, og, gains, q, k, v, both, cos, sin, allowed, *wo),
        "v" * 12 + "a" * 6,
        [
            pltpu.VMEM((4,) + wo[0].shape, BF),
            pltpu.VMEM((length, 4 * qw), BF),
            pltpu.VMEM((length, pad_lanes(4 * qw)), F32),
            pltpu.VMEM((length, pad_lanes(4 * kw)), F32),
            pltpu.VMEM((length, pad_lanes(4 * kw)), F32),
            pltpu.VMEM((4, length, cols), BF),
            pltpu.SemaphoreType.DMA((6,)),
        ],
        2 * length * width * width,
    )


def input_kernel(qw, kw, *refs):
    x_ref, dhidden_ref, dqkv_ref, gains_ref = refs[:4]
    grad_ref, gain_ref, wq, wkv, sems = refs[16:]
    copies = fetch_blocks(refs[4:10], wq, sems) + fetch_blocks(refs[10:16], wkv, sems, 6)
    x = x_ref[...].astype(F32)
    inverse = lax.rsqrt(jnp.mean(x * x, -1, keepdims=True) + EPSILON)
    normed = x * inverse
    wait_all(copies)
    dn1 = None
    for j in range(4):
        at = 4 * qw + 2 * j * kw
        term = back_product(dqkv_ref[:, j * qw : (j + 1) * qw], wq[j])
        term = term + dot(dqkv_ref[:, at : at + 2 * kw], wkv[j, : 2 * kw, :])
        dn1 = term if dn1 is None else dn1 + term
    gain_ref[...] = jnp.sum(dn1 * normed, 0, keepdims=True)
    scaled = dn1 * gains_ref[0:1, :]
    back = inverse * (scaled - normed * jnp.mean(scaled * normed, -1, keepdims=True))
    grad_ref[...] = dhidden_ref[...] + back


def input_backward(x, dhidden, dqkv, gains, wq, wkv, qw, kw):
    width = x.shape[1]
    return call(
        functools.partial(input_kernel, qw, kw),
        (jax.ShapeDtypeStruct(x.shape, F32), jax.ShapeDtypeStruct((1, width), F32)),
        (x, dhidden, dqkv, gains, *wq, *wkv),
        "v" * 4 + "a" * 12,
        [
            pltpu.VMEM((4,) + wq[0].shape, BF),
            pltpu.VMEM((4,) + wkv[0].shape, BF),
            pltpu.SemaphoreType.DMA((12,)),
        ],
        2 * x.size * dqkv.shape[1],
    )


def mixed_kernel(g0, g1, g2, g3, *refs):
    dm_ref, rows_ref, d_s, sems = refs[6:]
    copies = fetch_down(refs[:6], d_s, sems)
    length = g0.shape[0]
    for k, g in enumerate((g0, g1, g2, g3)):
        rows_ref[k * length : (k + 1) * length, :] = g[...]
    wait_all(copies)
    dm_ref[...] = dot(rows_ref[...], d_s[...])


def mixed_backward(og_blocks, down):
    length, width = og_blocks[0].shape
    units = down[1].shape[1]
    return call(
        mixed_kernel,
        (jax.ShapeDtypeStruct((4 * length, units), F32), jax.ShapeDtypeStruct((4 * length, width), BF)),
        (*og_blocks, *down),
        "v" * 4 + "a" * 6,
        [pltpu.VMEM((width, units), BF), pltpu.SemaphoreType.DMA((6,))],
        8 * length * width * units,
    )


def mlp_kernel(
    n0, n1, n2, n3, dm_ref, gate_ref, up_ref, mixed_ref, dg_ref, du_ref, own_ref, far_ref, near_ref, n_ref,
):
    length = n0.shape[0]
    for k, n in enumerate((n0, n1, n2, n3)):
        n_ref[k * length : (k + 1) * length, :] = n[...]
    gate = dot(n_ref[...], gate_ref[...])
    up = dot(n_ref[...], up_ref[...])
    dm = dm_ref[...]
    sig = 1.0 / (1.0 + jnp.exp(-gate))
    swish = gate * sig
    mixed_ref[...] = (swish * up).astype(BF)
    dg = (dm * up * sig * (1.0 + gate * (1.0 - sig))).astype(BF)
    du = (dm * swish).astype(BF)
    dg_ref[...] = dg
    du_ref[...] = du
    total = back_product(dg, gate_ref[...]) + back_product(du, up_ref[...])
    own_ref[...] = total[:length]
    near_ref[0] = total[length : 2 * length].astype(BF)
    far_ref[...] = total[2 * length : 3 * length]
    near_ref[1] = total[3 * length :].astype(BF)


def mlp(n2_blocks, dm, gate, up):
    length, width = n2_blocks[0].shape
    units = gate.shape[1]
    hid = jax.ShapeDtypeStruct((4 * length, units), BF)
    one = jax.ShapeDtypeStruct((length, width), F32)
    return call(
        mlp_kernel,
        (
            hid, hid, hid, one, one, jax.ShapeDtypeStruct((2, length, width), BF),
            jax.ShapeDtypeStruct((4 * length, width), BF),
        ),
        (*n2_blocks, dm, gate, up),
        "v" * 7,
        [],
        32 * length * width * units,
    )


def output_kernel(mixed_ref, *refs):
    own_ref, far_ref, near_ref, d_s, sems = refs[6:]
    copies = fetch_down(refs[:6], d_s, sems)
    length = own_ref.shape[0]
    wait_all(copies)
    total = back_product(mixed_ref[...], d_s[...])
    own_ref[...] = total[:length]
    near_ref[0] = total[length : 2 * length].astype(BF)
    far_ref[...] = total[2 * length : 3 * length]
    near_ref[1] = total[3 * length :].astype(BF)


def output_parts(mixed, down):
    length = mixed.shape[0] // 4
    width = 4 * down[1].shape[0]
    one = jax.ShapeDtypeStruct((length, width), F32)
    return call(
        output_kernel,
        (one, one, jax.ShapeDtypeStruct((2, length, width), BF)),
        (mixed, *down),
        "v" + "a" * 6,
        [pltpu.VMEM((width, mixed.shape[1]), BF), pltpu.SemaphoreType.DMA((6,))],
        8 * length * width * mixed.shape[1],
    )


def split_store(total, rows, bits, first, target, columns):
    mine = jnp.bitwise_and(lax.shift_right_logical(lax.axis_index("replica"), first), 1)
    for r in range(1 << bits):
        side = jnp.bitwise_xor((r >> first) & 1, mine)
        place = (r & ((1 << first) - 1)) | ((r >> (first + 1)) << first)
        target[side, place, :, columns] = total[r * rows : (r + 1) * rows].astype(BF)


def gate_up_kernel(rows, bits, firsts, n_ref, dg_ref, du_ref, *refs):
    left = n_ref[...]
    scratch = refs[-1]
    for i, grad in enumerate((dg_ref, du_ref)):
        split_store(rows_product(left, grad[...]), rows, bits, firsts[i], scratch, slice(None))
        refs[2 * i][...] = scratch[0]
        refs[2 * i + 1][...] = scratch[1]


def attention_grads_kernel(rows, bits, firsts, qkv, width, *refs):
    keep0, send0, keep1, send1, scratch = refs[8:]
    both = jnp.concatenate([r[...] for r in refs[:4]], 0)
    grads = jnp.concatenate([r[...] for r in refs[4:8]], 0)
    base = both.shape[1] // 2
    cols = grads.shape[1]
    split_store(rows_product(both[:, :width], grads[:, :qkv]), rows, bits, firsts[0], scratch, slice(0, qkv))
    keep0[...] = scratch[0, :, :, :qkv]
    send0[...] = scratch[1, :, :, :qkv]
    other = slice(0, cols - qkv)
    split_store(
        rows_product(both[:, base : base + width], grads[:, qkv:]), rows, bits, firsts[1], scratch, other
    )
    keep1[...] = scratch[0, :, :, other]
    send1[...] = scratch[1, :, :, other]


def split_grads(kernel, args, width, cols, firsts, replicas, *more):
    rows = width // replicas
    piece = lambda c: jax.ShapeDtypeStruct((replicas // 2, rows, c), BF)
    out = call(
        functools.partial(kernel, rows, replicas.bit_length() - 1, firsts, *more),
        tuple(piece(c) for c in cols for _ in range(2)),
        args,
        "v" * len(args),
        [pltpu.VMEM((2,) + piece(max(cols)).shape, BF)],
        2 * width * sum(cols) * 4 * args[0].shape[0],
    )
    return [out[2 * i : 2 * i + 2] for i in range(len(cols))]


def down_part_kernel(mixed_ref, og_ref, own_ref, near_ref, far_ref, diag_ref, d_s):
    me = lax.axis_index("fsdp")
    qw = own_ref.shape[1]
    total = rows_product(mixed_ref[...], og_ref[...])
    for j in range(4):
        d_s[jnp.bitwise_xor(me, j)] = total[:, j * qw : (j + 1) * qw].astype(BF)
    own_ref[...] = d_s[0]
    near_ref[...] = d_s[1]
    far_ref[...] = d_s[2]
    diag_ref[...] = d_s[3]


def down_parts(mixed, og_rows):
    units, width = mixed.shape[1], og_rows.shape[1]
    one = jax.ShapeDtypeStruct((units, width // 4), BF)
    return call(
        down_part_kernel, (one,) * 4, (mixed, og_rows), "vv", [pltpu.VMEM((4,) + one.shape, BF)], 2 * mixed.size * width
    )


def down_split_kernel(rows, first, b0, b1, b2, b3, keep, send, scratch):
    me = lax.axis_index("fsdp")
    mine = jnp.bitwise_and(lax.shift_right_logical(lax.axis_index("replica"), first), 1)
    per = b0.shape[0] // rows
    for k, block in enumerate((b0, b1, b2, b3)):
        for i in range(per):
            r = jnp.bitwise_xor(me, k) * per + i
            side = jnp.bitwise_xor(jnp.bitwise_and(lax.shift_right_logical(r, first), 1), mine)
            low = jnp.bitwise_and(r, (1 << first) - 1)
            place = jnp.bitwise_or(low, lax.shift_left(lax.shift_right_logical(r, first + 1), first))
            scratch[side, place] = block[i * rows : (i + 1) * rows, :]
    keep[...] = scratch[0]
    send[...] = scratch[1]


def down_split(blocks, first, replicas):
    rows = 4 * blocks[0].shape[0] // replicas
    piece = jax.ShapeDtypeStruct((replicas // 2, rows, blocks[0].shape[1]), BF)
    return call(
        functools.partial(down_split_kernel, rows, first),
        (piece, piece),
        blocks,
        "vvvv",
        [pltpu.VMEM((2,) + piece.shape, BF)],
    )


def fold_kernel(left, bit, keep_ref, came_ref, keep_out, send_out):
    mine = jnp.bitwise_and(lax.shift_right_logical(lax.axis_index("replica"), bit), 1)
    at = left.index(bit)
    for i in range(keep_out.shape[0]):
        base = (i & ((1 << at) - 1)) | ((i >> at) << (at + 1))
        for target, side in ((keep_out, mine), (send_out, 1 - mine)):
            place = base + lax.shift_left(side, at)
            target[i] = (keep_ref[place].astype(F32) + came_ref[place].astype(F32)).astype(BF)


def fold(keep, came, left, bit):
    piece = jax.ShapeDtypeStruct((keep.shape[0] // 2,) + keep.shape[1:], BF)
    return call(functools.partial(fold_kernel, tuple(left), bit), (piece, piece), (keep, came), "vv", [])


def fold_last_kernel(widths, turned, keep_ref, came_ref, *outs):
    total = keep_ref[0].astype(F32) + came_ref[0].astype(F32)
    at = 0
    for width, turn, out in zip(widths, turned, outs):
        part = total[:, at : at + width]
        out[...] = part.T if turn else part
        at += width


def fold_last(keep, came, widths, turned):
    rows = keep.shape[1]
    return call(
        functools.partial(fold_last_kernel, widths, turned),
        tuple(jax.ShapeDtypeStruct((w, rows) if t else (rows, w), F32) for w, t in zip(widths, turned)),
        (keep, came),
        "vv",
        [],
    )


def local(
    replicas,
    block_input,
    attn_gain,
    query_weight,
    key_matrix,
    value_matrix,
    output_weight,
    mlp_gain,
    gate_weight,
    up_weight,
    down_weight,
    segment_ids,
    out_grad,
):
    me = lax.axis_index("fsdp")
    _, width = block_input.shape[1:]
    qw, kw = query_weight.shape[1], key_matrix.shape[1]
    hidden_units = gate_weight.shape[1]
    og = out_grad[0]

    x = block_input[0]

    turned = down_weight.T
    kvg, q_half, kv_half, ow_half, dw_half, dw_near = pack(
        query_weight, output_weight, turned, key_matrix.T, value_matrix.T, attn_gain, mlp_gain
    )
    wq = gather_halves(query_weight, q_half, replicas)
    wkv = gather_halves(kvg, kv_half, replicas)
    wo = gather_halves(output_weight, ow_half, replicas)
    far_a = swap_fsdp(dw_half, 2)
    far_b = swap_replica(far_a, 1, replicas)
    near = swap_fsdp(dw_near, 1)
    diag_a = swap_fsdp(far_a, 1)
    diag_b = swap_fsdp(far_b, 1)
    down = [turned, near, far_a, far_b, diag_a, diag_b]
    og_all = gather_group(og)

    both, q, k, v, gains_all, cosine, sine, allowed = attention_forward(x, segment_ids, wq, wkv, qw, kw)
    hidden, n2 = hidden_forward(both, x, gains_all, wo)

    n2_all = gather_group(n2)
    dm, og_rows = mixed_backward(og_all, down)
    mixed, dg, du, dn2_own, dn2_far, dn2_near, n2_rows = mlp(n2_all, dm, gate_weight, up_weight)
    dn2_a, dn2_b = scatter_parts(dn2_own, dn2_far, dn2_near)
    both_all = gather_group(both)

    bits = replicas.bit_length() - 1
    first = [0] + list(range(1, bits))
    second = list(range(1, bits))
    second.insert(1, 0)
    gate_pair, up_pair = split_grads(
        gate_up_kernel, (n2_rows, dg, du), width, (hidden_units, hidden_units),
        (first[0], second[0]), replicas,
    )
    down_blocks = exchange_four(*down_parts(mixed, og_rows))
    down_pair = down_split(down_blocks, second[0], replicas)
    (gate_total,) = scatter_replica(gate_pair, first, replicas, (hidden_units,), (False,))
    (up_total,) = scatter_replica(up_pair, second, replicas, (hidden_units,), (False,))
    (down_total,) = scatter_replica(down_pair, second, replicas, (qw,), (False,))

    dhidden, mlp_gain_part, dx0, dx1, dx23, dqkv = attention_backward(
        dn2_a, dn2_b, hidden, og, gains_all, q, k, v, both, cosine, sine, allowed, wo, qw, kw,
    )
    dx_all = exchange_parts(dx0, dx1, dx23)
    input_grad, attn_gain_part = input_backward(x, dhidden, dqkv, gains_all, wq, wkv, qw, kw)
    qkv_pair, out_pair = split_grads(
        attention_grads_kernel, (*both_all, *dx_all), width, (qw + 2 * kw, qw),
        (first[0], second[0]), replicas, qw + 2 * kw, width,
    )
    query_total, key_total, value_total = scatter_replica(qkv_pair, first, replicas, (qw, kw, kw), (False, True, True))
    (out_total,) = scatter_replica(out_pair, second, replicas, (qw,), (False,))

    bo_a, bo_b = scatter_parts(*output_parts(mixed, down))
    result = (hidden + (bo_a + bo_b.astype(F32))).astype(BF)[None]
    input_grad = input_grad[None]

    total = jnp.concatenate([attn_gain_part, mlp_gain_part], 0)
    for bit in (1, 0):
        total = total + swap_fsdp(total, 1 << bit)
    for bit in [0] + list(range(bits - 1, 0, -1)):
        total = total + swap_replica(total, 1 << bit, replicas)
    total = lax.dynamic_slice_in_dim(total, me * qw, qw, 1)
    return (
        result,
        input_grad,
        total[0],
        query_total,
        key_total.T,
        value_total.T,
        out_total,
        total[1],
        gate_total,
        up_total,
        down_total,
    )


def solution(mesh):
    replicas = mesh.shape["replica"]

    def body(*args):
        return local(replicas, *args)

    rows = P(("fsdp", "replica"), None, None)
    cols = P(None, "fsdp")
    both = P("replica", "fsdp")
    return jax.shard_map(
        body,
        mesh=mesh,
        in_specs=(
            rows, P("fsdp"), cols, cols, cols, cols, P("fsdp"), cols, cols, cols,
            P(("fsdp", "replica"), None), rows,
        ),
        out_specs=(rows, rows, P("fsdp"), both, both, both, both, P("fsdp"), both, both, both),
        check_vma=False,
    )
```

```python
import functools
import math

import jax
import jax.numpy as jnp
from jax import lax
from jax.experimental import pallas as pl
from jax.experimental.pallas import tpu as pltpu
from jax.sharding import PartitionSpec as P


HEAD_DIMENSION = 64
EPSILON = 1e-05
ROPE_BASE = 100000.0
BF = jnp.bfloat16
F32 = jnp.float32


def dot(left, right):
    return jnp.dot(left, right, preferred_element_type=F32)


def rows_product(left, right):
    return lax.dot_general(left, right, (((0,), (0,)), ((), ())), preferred_element_type=F32)


def back_product(left, weight):
    return lax.dot_general(left, weight, (((1,), (1,)), ((), ())), preferred_element_type=F32)


def swap_fsdp(value, bit):
    return lax.ppermute(value, "fsdp", [(i, i ^ bit) for i in range(4)])


def swap_replica(value, bit, count):
    return lax.ppermute(value, "replica", [(i, i ^ bit) for i in range(count)])


def gather_group(value):
    far = swap_fsdp(value, 2)
    near = swap_fsdp(value, 1)
    return [value, near, far, swap_fsdp(far, 1)]


def gather_halves(value, half, replicas):
    far_a = swap_fsdp(half, 2)
    near = swap_fsdp(value, 1)
    far_b = swap_replica(far_a, 1, replicas)
    return [
        value, near, far_a, far_b,
        swap_fsdp(far_a, 1), swap_fsdp(far_b, 1),
    ]


def exchange_parts(own, near, far):
    came = swap_fsdp(far, 2)
    return [own, swap_fsdp(near, 1), came[0], swap_fsdp(came[1], 1)]


def exchange_four(own, near, far, diagonal):
    came = swap_fsdp(far, 2)
    passed = swap_fsdp(diagonal, 2)
    return [own, swap_fsdp(near, 1), came, swap_fsdp(passed, 1)]


def scatter_parts(own, far, near):
    came = swap_fsdp(near, 1).astype(F32)
    other = swap_fsdp((far + came[1]).astype(BF), 2)
    return own + came[0], other


def scatter_steps(pair, order, replicas):
    keep, send = pair
    left = sorted(order)
    for step, bit in enumerate(order):
        left.remove(bit)
        came = swap_replica(send, 1 << bit, replicas)
        if not left:
            return keep, came
        keep, send = fold(keep, came, left, order[step + 1])


def scatter_replica(pair, order, replicas, widths, turned):
    keep, came = scatter_steps(pair, order, replicas)
    return fold_last(keep, came, widths, turned)


def rotary_tables(earlier):
    lanes = lax.broadcasted_iota(jnp.int32, (1, 128), 1)
    half_size = HEAD_DIMENSION // 2
    index = (lanes % half_size).astype(F32)
    frequency = jnp.exp(index * (-2.0 * math.log(ROPE_BASE) / HEAD_DIMENSION))
    angles = earlier * frequency
    sine = jnp.sin(angles)
    return jnp.cos(angles), jnp.where(lanes % HEAD_DIMENSION < half_size, -sine, sine)


SPARE = 3 << 20
VMEM_SPEC = pl.BlockSpec(memory_space=pltpu.VMEM)
HBM_SPEC = pl.BlockSpec(memory_space=pltpu.HBM)


def call(kernel, out_shape, args, spaces, scratch, flops=0):
    bytes_accessed = sum(a.size * a.dtype.itemsize for a in list(args) + jax.tree.leaves(out_shape))
    size = lambda a: math.prod(a.shape[:-1]) * pad_lanes(a.shape[-1]) * jnp.dtype(a.dtype).itemsize
    held = [a for a, c in zip(args, spaces) if c == "v"] + jax.tree.leaves(out_shape)
    held += [a for a in scratch if isinstance(a, type(pltpu.VMEM((8, 128), F32))) and len(a.shape) > 1]
    room = sum(size(a) for a in held) + SPARE
    args = [pltpu.with_memory_space_constraint(a, pltpu.HBM) if c == "h" else a for a, c in zip(args, spaces)]
    return pl.pallas_call(
        kernel,
        out_shape=out_shape,
        in_specs=[VMEM_SPEC if c == "v" else HBM_SPEC for c in spaces],
        out_specs=jax.tree.map(lambda _: VMEM_SPEC, out_shape),
        scratch_shapes=scratch,
        cost_estimate=pl.CostEstimate(flops=flops, transcendentals=0, bytes_accessed=bytes_accessed),
        compiler_params=pltpu.CompilerParams(vmem_limit_bytes=room),
    )(*args)


def start_all(pairs, sems, base=0):
    copies = [pltpu.make_async_copy(a, b, sems.at[base + i]) for i, (a, b) in enumerate(pairs)]
    for copy in copies:
        copy.start()
    return copies


def wait_all(copies):
    for copy in copies:
        copy.wait()


def half_places(rows):
    parity = jnp.bitwise_and(lax.axis_index("replica"), 1)
    half = half_rows(rows)
    rest = rows - half
    start_a = pl.multiple_of(parity * rest, 16)
    skip = pl.multiple_of((1 - parity) * (half - rest), 16)
    start_b = pl.multiple_of((1 - parity) * half, 16)
    return pl.ds(start_a, half), pl.ds(skip, rest), pl.ds(start_b, rest)


def fetch_blocks(sources, target, sems, base=0):
    me = lax.axis_index("fsdp")
    own, near, far_a, far_b, diag_a, diag_b = sources
    a_at, b_from, b_at = half_places(own.shape[0])
    block = [target.at[jnp.bitwise_xor(me, k)] for k in range(4)]
    pairs = [(own, block[0]), (near, block[1])]
    for k, a, b in ((2, far_a, far_b), (3, diag_a, diag_b)):
        pairs += [(a, block[k].at[a_at]), (b.at[b_from], block[k].at[b_at])]
    return start_all(pairs, sems, base)


def half_rows(rows):
    return -(-rows // 32) * 16


def fetch_down(sources, target, sems):
    me = lax.axis_index("fsdp")
    own, near, far_a, far_b, diag_a, diag_b = sources
    rows, units = near.shape
    a_at, b_from, b_at = half_places(rows)
    core = pl.multiple_of(jnp.bitwise_and(me, 1) * units, units)
    block = [target.at[pl.ds(pl.multiple_of(jnp.bitwise_xor(me, k) * rows, rows), rows)] for k in range(4)]
    return start_all(
        [
            (own.at[:, pl.ds(pl.multiple_of(me * units, units), units)], block[0]),
            (near, block[1]),
            (far_a.at[:, pl.ds(core, units)], block[2].at[a_at]),
            (far_b.at[b_from, pl.ds(core, units)], block[2].at[b_at]),
            (diag_a.at[:, pl.ds(core, units)], block[3].at[a_at]),
            (diag_b.at[b_from, pl.ds(core, units)], block[3].at[b_at]),
        ],
        sems,
    )


def swap_halves(values):
    lanes = values.shape[1]
    half = HEAD_DIMENSION // 2
    index = lax.broadcasted_iota(jnp.int32, values.shape, 1)
    return jnp.where(
        index % HEAD_DIMENSION < half, pltpu.roll(values, lanes - half, 1), pltpu.roll(values, half, 1)
    )


def widen(table, lanes):
    return jnp.concatenate([table] * (lanes // table.shape[1]), 1)


def allowed_pairs(segments):
    length = segments.shape[1]
    row = lax.broadcasted_iota(jnp.int32, (length, length), 0)
    col = lax.broadcasted_iota(jnp.int32, (length, length), 1)
    keys = jnp.broadcast_to(segments.astype(F32), (length, length))
    return jnp.where((keys == keys.T) & (row >= col), 1.0, 0.0)


def heads_of(ref, group, ratio, base=0):
    d = HEAD_DIMENSION
    starts = [base + (group * ratio + r) * d for r in range(ratio)]
    return jnp.concatenate([ref[:, a : a + d] for a in starts], 0)


def probabilities(queries, keys, mask):
    scores = back_product(queries, keys) * (1.0 / math.sqrt(HEAD_DIMENSION))
    scores = jnp.where(mask, scores, -1e30)
    top = jnp.max(scores, -1, keepdims=True)
    total = top + jnp.log(jnp.sum(jnp.exp(scores - top), -1, keepdims=True))
    return jnp.exp(scores - total)


def half_start(rows):
    parity = jnp.bitwise_and(lax.axis_index("replica"), 1)
    return pl.multiple_of(parity * (rows - half_rows(rows)), 16)


def pack_kernel(
    q_ref, ow_ref, dw_ref, k_ref, v_ref, ga_ref, gm_ref, kv_ref, q_half, kv_half, ow_half, dw_half, dw_near,
    ga_s, gm_s, sems,
):
    me = lax.axis_index("fsdp")
    units = dw_near.shape[1]
    rows_of = lambda full, half: pl.ds(half_start(full.shape[0]), half.shape[0])
    across = pl.multiple_of((1 - lax.shift_right_logical(me, 1)) * 2 * units, 128)
    mate = pl.multiple_of(jnp.bitwise_xor(me, 1) * units, 128)
    kw = k_ref.shape[0]
    qw = ga_ref.shape[0]
    small = [
        (k_ref, kv_ref.at[pl.ds(0, kw)]),
        (v_ref, kv_ref.at[pl.ds(kw, kw)]),
        (ga_ref, ga_s),
        (gm_ref, gm_s),
    ]
    large = [
        (q_ref.at[rows_of(q_ref, q_half)], q_half),
        (ow_ref.at[rows_of(ow_ref, ow_half)], ow_half),
        (dw_ref.at[rows_of(dw_ref, dw_half), pl.ds(across, 2 * units)], dw_half),
        (dw_ref.at[:, pl.ds(mate, units)], dw_near),
    ]
    small, large = start_all(small, sems), start_all(large, sems, len(small))
    wait_all(small)
    row = lax.broadcasted_iota(jnp.int32, (16, qw), 0)
    first, second = (jnp.broadcast_to(r[...].astype(F32)[None, :], (16, qw)) for r in (ga_s, gm_s))
    kv_ref[2 * kw :, :] = jnp.zeros((16, kv_ref.shape[1]), BF)
    kv_ref[2 * kw :, :qw] = jnp.where(row == 0, first, second).astype(BF)
    half = kv_half.shape[0]
    parity = jnp.bitwise_and(lax.axis_index("replica"), 1)

    @pl.when(parity == 0)
    def _():
        kv_half[...] = kv_ref[:half, :]

    @pl.when(parity == 1)
    def _():
        kv_half[...] = kv_ref[kv_ref.shape[0] - half :, :]

    wait_all(large)


def pack(query_weight, output_weight, turned, keys, values, attn_gain, mlp_gain):
    width, qw = query_weight.shape
    kw = keys.shape[0]
    units = turned.shape[1] // 4
    f = lambda *shape: jax.ShapeDtypeStruct(shape, BF)
    return call(
        pack_kernel,
        (
            f(2 * kw + 16, width), f(half_rows(width), qw), f(half_rows(2 * kw + 16), width),
            f(half_rows(output_weight.shape[0]), qw), f(half_rows(qw), 2 * units), f(qw, units),
        ),
        (query_weight, output_weight, turned, keys, values, attn_gain, mlp_gain),
        "h" * 7,
        [pltpu.VMEM((qw,), BF), pltpu.VMEM((qw,), BF), pltpu.SemaphoreType.DMA((8,))],
    )


def attention_kernel(qw, kw, *refs):
    x_ref, segments_ref = refs[:2]
    both_ref, q_ref, k_ref, v_ref, gains_ref, cos_ref, sin_ref, prob_ref, wq, wkv, q_s, k_s, sems = refs[14:]
    copies = fetch_blocks(refs[2:8], wq, sems) + fetch_blocks(refs[8:14], wkv, sems, 6)
    allowed = allowed_pairs(segments_ref[...])
    cos_ref[...], sin_ref[...] = rotary_tables(jnp.sum(allowed, -1, keepdims=True) - 1.0)
    groups = 4 * kw // HEAD_DIMENSION
    ratio = qw // kw
    x = x_ref[...].astype(F32)
    normed = x * lax.rsqrt(jnp.mean(x * x, -1, keepdims=True) + EPSILON)
    mask = jnp.concatenate([allowed] * ratio, 0) > 0.5
    wait_all(copies)
    for j in range(4):
        gains_ref[:, j * qw : (j + 1) * qw] = wkv[j, 2 * kw : 2 * kw + 16, :qw].astype(F32)
    n1 = (normed * gains_ref[0:1, :]).astype(BF)
    width = x_ref.shape[1]
    base = both_ref.shape[1] // 2
    both_ref[:, :width] = n1
    for j in range(4):
        q_s[:, j * qw : (j + 1) * qw] = dot(n1, wq[j])
        two = back_product(n1, wkv[j, : 2 * kw, :])
        k_s[:, j * kw : (j + 1) * kw] = two[:, :kw]
        v_ref[:, j * kw : (j + 1) * kw] = two[:, kw:].astype(BF)
    for source, target in ((q_s, q_ref), (k_s, k_ref)):
        values = source[...]
        lanes = values.shape[1]
        turned = values * widen(cos_ref[...], lanes) + swap_halves(values) * widen(sin_ref[...], lanes)
        target[...] = turned[:, : target.shape[1]].astype(BF)
    length = x_ref.shape[0]
    d = HEAD_DIMENSION
    for g in range(groups):
        prob = probabilities(heads_of(q_ref, g, ratio), k_ref[:, g * d : (g + 1) * d], mask).astype(BF)
        prob_ref[g] = prob
        out = dot(prob, v_ref[:, g * d : (g + 1) * d]).astype(BF)
        for r in range(ratio):
            h = g * ratio + r
            both_ref[:, base + h * d : base + (h + 1) * d] = out[r * length : (r + 1) * length]


def pad_lanes(n):
    return -(-n // 128) * 128


def attention_forward(x, segments, wq, wkv, qw, kw):
    length, width = x.shape
    f = lambda *shape: jax.ShapeDtypeStruct(shape, BF)
    return call(
        functools.partial(attention_kernel, qw, kw),
        (
            f(length, 2 * pad_lanes(width)), f(length, 4 * qw), f(length, 4 * kw), f(length, 4 * kw),
            jax.ShapeDtypeStruct((16, width), F32),
            jax.ShapeDtypeStruct((length, 128), F32),
            jax.ShapeDtypeStruct((length, 128), F32),
            f(4 * kw // HEAD_DIMENSION, qw // kw * length, length),
            f(4, *wq[0].shape),
            f(4, *wkv[0].shape),
        ),
        (x, segments, *wq, *wkv),
        "v" * 2 + "a" * 12,
        [
            pltpu.VMEM((length, pad_lanes(4 * qw)), F32),
            pltpu.VMEM((length, pad_lanes(4 * kw)), F32),
            pltpu.SemaphoreType.DMA((12,)),
        ],
        2 * length * width * 4 * (qw + 2 * kw),
    )


def hidden_kernel(*refs):
    both_ref, x_ref, gains_ref = refs[:3]
    hidden_ref, n2_ref, w_s, sems = refs[9:]
    copies = fetch_blocks(refs[3:9], w_s, sems)
    qw = w_s.shape[2]
    base = both_ref.shape[1] // 2
    attended = both_ref[:, base : base + x_ref.shape[1]]
    wait_all(copies)
    for j in range(4):
        part = slice(j * qw, (j + 1) * qw)
        hidden_ref[:, part] = x_ref[:, part].astype(F32) + dot(attended, w_s[j])
    hidden = hidden_ref[...]
    normed = hidden * lax.rsqrt(jnp.mean(hidden * hidden, -1, keepdims=True) + EPSILON)
    n2_ref[...] = (normed * gains_ref[1:2, :]).astype(BF)


def hidden_forward(both, x, gains, wo):
    return call(
        hidden_kernel,
        (
            jax.ShapeDtypeStruct(x.shape, F32),
            jax.ShapeDtypeStruct(x.shape, BF),
            jax.ShapeDtypeStruct((4,) + wo[0].shape, BF),
        ),
        (both, x, gains, *wo),
        "v" * 3 + "a" * 6,
        [pltpu.SemaphoreType.DMA((6,))],
        2 * x.size * x.shape[1],
    )


def backward_kernel(qw, kw, *refs):
    (dn2_a, dn2_b, hidden_ref, og_ref, gains_ref, q_ref, k_ref, v_ref, both_ref, cos_ref,
     sin_ref, prob_ref, w_s) = refs[:13]
    (dhidden_ref, gain_ref, dx0, dx1, dx23, dqkv_ref, do_s, dq_s, dk_s, dv_s, x_s) = refs[13:]
    base = both_ref.shape[1] // 2
    cols = qw + 2 * kw
    me = lax.axis_index("fsdp")
    length = hidden_ref.shape[0]
    d = HEAD_DIMENSION
    groups = 4 * kw // d
    ratio = qw // kw
    dn2 = dn2_a[...] + dn2_b[...].astype(F32)
    hidden = hidden_ref[...]
    inverse = lax.rsqrt(jnp.mean(hidden * hidden, -1, keepdims=True) + EPSILON)
    normed = hidden * inverse
    gain_ref[...] = jnp.sum(dn2 * normed, 0, keepdims=True)
    scaled = dn2 * gains_ref[1:2, :]
    back = inverse * (scaled - normed * jnp.mean(scaled * normed, -1, keepdims=True))
    dhidden = og_ref[...].astype(F32) + back
    dhidden_ref[...] = dhidden
    db = dhidden.astype(BF)
    do = None
    for j in range(4):
        part = db[:, j * qw : (j + 1) * qw]
        x_s[jnp.bitwise_xor(me, j), :, cols:] = part
        term = back_product(part, w_s[j])
        do = term if do is None else do + term
    do_s[...] = do.astype(BF)
    for g in range(groups):
        at = slice(g * d, (g + 1) * d)
        queries = heads_of(q_ref, g, ratio)
        keys = k_ref[:, at]
        soft = prob_ref[g]
        grad = heads_of(do_s, g, ratio)
        dv_s[:, at] = rows_product(soft, grad)
        dp = back_product(grad, v_ref[:, at])
        delta = jnp.sum(grad.astype(F32) * heads_of(both_ref, g, ratio, base).astype(F32), -1, keepdims=True)
        ds = (soft.astype(F32) * (dp - delta) * (1.0 / math.sqrt(d))).astype(BF)
        dq = dot(ds, keys)
        for r in range(ratio):
            h = g * ratio + r
            dq_s[:, h * d : (h + 1) * d] = dq[r * length : (r + 1) * length]
        dk_s[:, at] = rows_product(ds, queries)
    for ref in (dq_s, dk_s):
        values = ref[...]
        lanes = values.shape[1]
        ref[...] = values * widen(cos_ref[...], lanes) - swap_halves(values) * widen(sin_ref[...], lanes)
    dqkv_ref[:, : 4 * qw] = dq_s[:, : 4 * qw].astype(BF)
    for j in range(4):
        k_at = 4 * qw + 2 * j * kw
        dqkv_ref[:, k_at : k_at + kw] = dk_s[:, j * kw : (j + 1) * kw].astype(BF)
        dqkv_ref[:, k_at + kw : k_at + 2 * kw] = dv_s[:, j * kw : (j + 1) * kw].astype(BF)
        at = jnp.bitwise_xor(me, j)
        x_s[at, :, :qw] = dq_s[:, j * qw : (j + 1) * qw].astype(BF)
        x_s[at, :, qw : qw + kw] = dk_s[:, j * kw : (j + 1) * kw].astype(BF)
        x_s[at, :, qw + kw : cols] = dv_s[:, j * kw : (j + 1) * kw].astype(BF)
    dx0[...] = x_s[0]
    dx1[...] = x_s[1]
    dx23[...] = x_s[2:4]


def attention_backward(dn2_a, dn2_b, hidden, og, gains, q, k, v, both, cos, sin, prob, wo, qw, kw):
    length, width = hidden.shape
    cols = 2 * qw + 2 * kw
    f = lambda *shape: jax.ShapeDtypeStruct(shape, BF)
    return call(
        functools.partial(backward_kernel, qw, kw),
        (
            jax.ShapeDtypeStruct(hidden.shape, F32),
            jax.ShapeDtypeStruct((1, width), F32),
            f(length, cols), f(length, cols), f(2, length, cols),
            f(length, 4 * (qw + 2 * kw)),
        ),
        (dn2_a, dn2_b, hidden, og, gains, q, k, v, both, cos, sin, prob, wo),
        "v" * 13,
        [
            pltpu.VMEM((length, 4 * qw), BF),
            pltpu.VMEM((length, pad_lanes(4 * qw)), F32),
            pltpu.VMEM((length, pad_lanes(4 * kw)), F32),
            pltpu.VMEM((length, pad_lanes(4 * kw)), F32),
            pltpu.VMEM((4, length, cols), BF),
        ],
        2 * length * width * width,
    )


def input_kernel(qw, kw, *refs):
    x_ref, dhidden_ref, dqkv_ref, gains_ref, wq, wkv, grad_ref, gain_ref = refs
    x = x_ref[...].astype(F32)
    inverse = lax.rsqrt(jnp.mean(x * x, -1, keepdims=True) + EPSILON)
    normed = x * inverse
    dn1 = None
    for j in range(4):
        at = 4 * qw + 2 * j * kw
        term = back_product(dqkv_ref[:, j * qw : (j + 1) * qw], wq[j])
        term = term + dot(dqkv_ref[:, at : at + 2 * kw], wkv[j, : 2 * kw, :])
        dn1 = term if dn1 is None else dn1 + term
    gain_ref[...] = jnp.sum(dn1 * normed, 0, keepdims=True)
    scaled = dn1 * gains_ref[0:1, :]
    back = inverse * (scaled - normed * jnp.mean(scaled * normed, -1, keepdims=True))
    grad_ref[...] = dhidden_ref[...] + back


def input_backward(x, dhidden, dqkv, gains, wq, wkv, qw, kw):
    width = x.shape[1]
    return call(
        functools.partial(input_kernel, qw, kw),
        (jax.ShapeDtypeStruct(x.shape, F32), jax.ShapeDtypeStruct((1, width), F32)),
        (x, dhidden, dqkv, gains, wq, wkv),
        "v" * 6,
        [],
        2 * x.size * dqkv.shape[1],
    )


def mixed_kernel(g0, g1, g2, g3, *refs):
    dm_ref, rows_ref, d_s, sems = refs[6:]
    copies = fetch_down(refs[:6], d_s, sems)
    length = g0.shape[0]
    for k, g in enumerate((g0, g1, g2, g3)):
        rows_ref[k * length : (k + 1) * length, :] = g[...]
    wait_all(copies)
    dm_ref[...] = dot(rows_ref[...], d_s[...])


def mixed_backward(og_blocks, down):
    length, width = og_blocks[0].shape
    units = down[1].shape[1]
    return call(
        mixed_kernel,
        (
            jax.ShapeDtypeStruct((4 * length, units), F32),
            jax.ShapeDtypeStruct((4 * length, width), BF),
            jax.ShapeDtypeStruct((width, units), BF),
        ),
        (*og_blocks, *down),
        "v" * 4 + "a" * 6,
        [pltpu.SemaphoreType.DMA((6,))],
        8 * length * width * units,
    )


def mlp_kernel(
    n0, n1, n2, n3, dm_ref, gate_ref, up_ref, mixed_ref, dg_ref, du_ref, own_ref, far_ref, near_ref, n_ref,
):
    length = n0.shape[0]
    for k, n in enumerate((n0, n1, n2, n3)):
        n_ref[k * length : (k + 1) * length, :] = n[...]
    gate = dot(n_ref[...], gate_ref[...])
    up = dot(n_ref[...], up_ref[...])
    dm = dm_ref[...]
    sig = 1.0 / (1.0 + jnp.exp(-gate))
    swish = gate * sig
    mixed_ref[...] = (swish * up).astype(BF)
    dg = (dm * up * sig * (1.0 + gate * (1.0 - sig))).astype(BF)
    du = (dm * swish).astype(BF)
    dg_ref[...] = dg
    du_ref[...] = du
    total = back_product(dg, gate_ref[...]) + back_product(du, up_ref[...])
    own_ref[...] = total[:length]
    near_ref[0] = total[length : 2 * length].astype(BF)
    far_ref[...] = total[2 * length : 3 * length]
    near_ref[1] = total[3 * length :].astype(BF)


def mlp(n2_blocks, dm, gate, up):
    length, width = n2_blocks[0].shape
    units = gate.shape[1]
    hid = jax.ShapeDtypeStruct((4 * length, units), BF)
    one = jax.ShapeDtypeStruct((length, width), F32)
    return call(
        mlp_kernel,
        (
            hid, hid, hid, one, one, jax.ShapeDtypeStruct((2, length, width), BF),
            jax.ShapeDtypeStruct((4 * length, width), BF),
        ),
        (*n2_blocks, dm, gate, up),
        "v" * 7,
        [],
        32 * length * width * units,
    )


def output_kernel(mixed_ref, d_s, own_ref, far_ref, near_ref):
    length = own_ref.shape[0]
    total = back_product(mixed_ref[...], d_s[...])
    own_ref[...] = total[:length]
    near_ref[0] = total[length : 2 * length].astype(BF)
    far_ref[...] = total[2 * length : 3 * length]
    near_ref[1] = total[3 * length :].astype(BF)


def output_parts(mixed, down):
    length = mixed.shape[0] // 4
    width = down.shape[0]
    one = jax.ShapeDtypeStruct((length, width), F32)
    return call(
        output_kernel,
        (one, one, jax.ShapeDtypeStruct((2, length, width), BF)),
        (mixed, down),
        "vv",
        [],
        8 * length * width * mixed.shape[1],
    )


def split_store(total, rows, bits, first, target, columns):
    mine = jnp.bitwise_and(lax.shift_right_logical(lax.axis_index("replica"), first), 1)
    for r in range(1 << bits):
        side = jnp.bitwise_xor((r >> first) & 1, mine)
        place = (r & ((1 << first) - 1)) | ((r >> (first + 1)) << first)
        target[side, place, :, columns] = total[r * rows : (r + 1) * rows].astype(BF)


def gate_up_kernel(rows, bits, firsts, n_ref, dg_ref, du_ref, *refs):
    left = n_ref[...]
    scratch = refs[-1]
    for i, grad in enumerate((dg_ref, du_ref)):
        split_store(rows_product(left, grad[...]), rows, bits, firsts[i], scratch, slice(None))
        refs[2 * i][...] = scratch[0]
        refs[2 * i + 1][...] = scratch[1]


def attention_grads_kernel(rows, bits, firsts, qkv, width, *refs):
    keep0, send0, keep1, send1, scratch = refs[8:]
    both = jnp.concatenate([r[...] for r in refs[:4]], 0)
    grads = jnp.concatenate([r[...] for r in refs[4:8]], 0)
    base = both.shape[1] // 2
    cols = grads.shape[1]
    split_store(rows_product(both[:, :width], grads[:, :qkv]), rows, bits, firsts[0], scratch, slice(0, qkv))
    keep0[...] = scratch[0, :, :, :qkv]
    send0[...] = scratch[1, :, :, :qkv]
    other = slice(0, cols - qkv)
    split_store(
        rows_product(both[:, base : base + width], grads[:, qkv:]), rows, bits, firsts[1], scratch, other
    )
    keep1[...] = scratch[0, :, :, other]
    send1[...] = scratch[1, :, :, other]


def split_grads(kernel, args, width, cols, firsts, replicas, *more):
    rows = width // replicas
    piece = lambda c: jax.ShapeDtypeStruct((replicas // 2, rows, c), BF)
    out = call(
        functools.partial(kernel, rows, replicas.bit_length() - 1, firsts, *more),
        tuple(piece(c) for c in cols for _ in range(2)),
        args,
        "v" * len(args),
        [pltpu.VMEM((2,) + piece(max(cols)).shape, BF)],
        2 * width * sum(cols) * 4 * args[0].shape[0],
    )
    return [out[2 * i : 2 * i + 2] for i in range(len(cols))]


def down_part_kernel(mixed_ref, og_ref, own_ref, near_ref, far_ref, diag_ref, d_s):
    me = lax.axis_index("fsdp")
    qw = own_ref.shape[1]
    total = rows_product(mixed_ref[...], og_ref[...])
    for j in range(4):
        d_s[jnp.bitwise_xor(me, j)] = total[:, j * qw : (j + 1) * qw].astype(BF)
    own_ref[...] = d_s[0]
    near_ref[...] = d_s[1]
    far_ref[...] = d_s[2]
    diag_ref[...] = d_s[3]


def down_parts(mixed, og_rows):
    units, width = mixed.shape[1], og_rows.shape[1]
    one = jax.ShapeDtypeStruct((units, width // 4), BF)
    return call(
        down_part_kernel, (one,) * 4, (mixed, og_rows), "vv", [pltpu.VMEM((4,) + one.shape, BF)], 2 * mixed.size * width
    )


def down_split_kernel(rows, firsts, b0, b1, b2, b3, keep0, send0, keep1, send1, half0, half1):
    me = lax.axis_index("fsdp")
    cut = keep0.shape[2]
    per = b0.shape[0] // rows
    for first, scratch, columns in ((firsts[0], half0, slice(0, cut)), (firsts[1], half1, slice(cut, None))):
        mine = jnp.bitwise_and(lax.shift_right_logical(lax.axis_index("replica"), first), 1)
        for k, block in enumerate((b0, b1, b2, b3)):
            for i in range(per):
                r = jnp.bitwise_xor(me, k) * per + i
                side = jnp.bitwise_xor(jnp.bitwise_and(lax.shift_right_logical(r, first), 1), mine)
                low = jnp.bitwise_and(r, (1 << first) - 1)
                place = jnp.bitwise_or(low, lax.shift_left(lax.shift_right_logical(r, first + 1), first))
                scratch[side, place] = block[i * rows : (i + 1) * rows, columns]
    keep0[...] = half0[0]
    send0[...] = half0[1]
    keep1[...] = half1[0]
    send1[...] = half1[1]


def down_split(blocks, firsts, replicas):
    rows = 4 * blocks[0].shape[0] // replicas
    cols = blocks[0].shape[1]
    cut = cols // 256 * 128 if cols >= 256 else 128
    pieces = [jax.ShapeDtypeStruct((replicas // 2, rows, c), BF) for c in (cut, cols - cut)]
    out = call(
        functools.partial(down_split_kernel, rows, firsts),
        (pieces[0], pieces[0], pieces[1], pieces[1]),
        blocks,
        "vvvv",
        [pltpu.VMEM((2,) + p.shape, BF) for p in pieces],
    )
    return out[:2], out[2:]


def join_kernel(keep0, came0, keep1, came1, out_ref):
    cut = keep0.shape[2]
    out_ref[:, :cut] = keep0[0].astype(F32) + came0[0].astype(F32)
    out_ref[:, cut:] = keep1[0].astype(F32) + came1[0].astype(F32)


def join(keep0, came0, keep1, came1):
    out = jax.ShapeDtypeStruct((keep0.shape[1], keep0.shape[2] + keep1.shape[2]), F32)
    return call(join_kernel, out, (keep0, came0, keep1, came1), "vvvv", [])


def fold_kernel(left, bit, keep_ref, came_ref, keep_out, send_out):
    mine = jnp.bitwise_and(lax.shift_right_logical(lax.axis_index("replica"), bit), 1)
    at = left.index(bit)
    for i in range(keep_out.shape[0]):
        base = (i & ((1 << at) - 1)) | ((i >> at) << (at + 1))
        for target, side in ((keep_out, mine), (send_out, 1 - mine)):
            place = base + lax.shift_left(side, at)
            target[i] = (keep_ref[place].astype(F32) + came_ref[place].astype(F32)).astype(BF)


def fold(keep, came, left, bit):
    piece = jax.ShapeDtypeStruct((keep.shape[0] // 2,) + keep.shape[1:], BF)
    return call(functools.partial(fold_kernel, tuple(left), bit), (piece, piece), (keep, came), "vv", [])


def fold_last_kernel(widths, turned, keep_ref, came_ref, *outs):
    total = keep_ref[0].astype(F32) + came_ref[0].astype(F32)
    at = 0
    for width, turn, out in zip(widths, turned, outs):
        part = total[:, at : at + width]
        out[...] = part.T if turn else part
        at += width


def fold_last(keep, came, widths, turned):
    rows = keep.shape[1]
    return call(
        functools.partial(fold_last_kernel, widths, turned),
        tuple(jax.ShapeDtypeStruct((w, rows) if t else (rows, w), F32) for w, t in zip(widths, turned)),
        (keep, came),
        "vv",
        [],
    )


def local(
    replicas,
    block_input,
    attn_gain,
    query_weight,
    key_matrix,
    value_matrix,
    output_weight,
    mlp_gain,
    gate_weight,
    up_weight,
    down_weight,
    segment_ids,
    out_grad,
):
    me = lax.axis_index("fsdp")
    _, width = block_input.shape[1:]
    qw, kw = query_weight.shape[1], key_matrix.shape[1]
    hidden_units = gate_weight.shape[1]
    og = out_grad[0]

    x = block_input[0]

    turned = down_weight.T
    kvg, q_half, kv_half, ow_half, dw_half, dw_near = pack(
        query_weight, output_weight, turned, key_matrix.T, value_matrix.T, attn_gain, mlp_gain
    )
    wq = gather_halves(query_weight, q_half, replicas)
    wkv = gather_halves(kvg, kv_half, replicas)
    wo = gather_halves(output_weight, ow_half, replicas)
    far_a = swap_fsdp(dw_half, 2)
    far_b = swap_replica(far_a, 1, replicas)
    near = swap_fsdp(dw_near, 1)
    diag_a = swap_fsdp(far_a, 1)
    diag_b = swap_fsdp(far_b, 1)
    down = [turned, near, far_a, far_b, diag_a, diag_b]
    og_all = gather_group(og)

    both, q, k, v, gains_all, cosine, sine, prob, wq_all, wkv_all = attention_forward(x, segment_ids, wq, wkv, qw, kw)
    hidden, n2, wo_all = hidden_forward(both, x, gains_all, wo)

    n2_all = gather_group(n2)
    dm, og_rows, down_rows = mixed_backward(og_all, down)
    mixed, dg, du, dn2_own, dn2_far, dn2_near, n2_rows = mlp(n2_all, dm, gate_weight, up_weight)
    dn2_a, dn2_b = scatter_parts(dn2_own, dn2_far, dn2_near)
    both_all = gather_group(both)

    bits = replicas.bit_length() - 1
    first = [0] + list(range(1, bits))
    second = list(range(1, bits))
    second.insert(1, 0)
    gate_pair, up_pair = split_grads(
        gate_up_kernel, (n2_rows, dg, du), width, (hidden_units, hidden_units),
        (first[0], second[0]), replicas,
    )
    down_blocks = exchange_four(*down_parts(mixed, og_rows))
    down_one, down_two = down_split(down_blocks, (first[0], second[0]), replicas)
    (gate_total,) = scatter_replica(gate_pair, first, replicas, (hidden_units,), (False,))
    (up_total,) = scatter_replica(up_pair, second, replicas, (hidden_units,), (False,))
    down_one = scatter_steps(down_one, first, replicas)
    down_total = join(*down_one, *scatter_steps(down_two, second, replicas))

    dhidden, mlp_gain_part, dx0, dx1, dx23, dqkv = attention_backward(
        dn2_a, dn2_b, hidden, og, gains_all, q, k, v, both, cosine, sine, prob, wo_all, qw, kw,
    )
    dx_all = exchange_parts(dx0, dx1, dx23)
    input_grad, attn_gain_part = input_backward(x, dhidden, dqkv, gains_all, wq_all, wkv_all, qw, kw)
    qkv_pair, out_pair = split_grads(
        attention_grads_kernel, (*both_all, *dx_all), width, (qw + 2 * kw, qw),
        (first[0], second[0]), replicas, qw + 2 * kw, width,
    )
    query_total, key_total, value_total = scatter_replica(qkv_pair, first, replicas, (qw, kw, kw), (False, True, True))
    (out_total,) = scatter_replica(out_pair, second, replicas, (qw,), (False,))

    bo_a, bo_b = scatter_parts(*output_parts(mixed, down_rows))
    result = (hidden + (bo_a + bo_b.astype(F32))).astype(BF)[None]
    input_grad = input_grad[None]

    total = jnp.concatenate([attn_gain_part, mlp_gain_part], 0)
    for bit in (1, 0):
        total = total + swap_fsdp(total, 1 << bit)
    for bit in [0] + list(range(bits - 1, 0, -1)):
        total = total + swap_replica(total, 1 << bit, replicas)
    total = lax.dynamic_slice_in_dim(total, me * qw, qw, 1)
    return (
        result,
        input_grad,
        total[0],
        query_total,
        key_total.T,
        value_total.T,
        out_total,
        total[1],
        gate_total,
        up_total,
        down_total,
    )


def solution(mesh):
    replicas = mesh.shape["replica"]

    def body(*args):
        return local(replicas, *args)

    rows = P(("fsdp", "replica"), None, None)
    cols = P(None, "fsdp")
    both = P("replica", "fsdp")
    return jax.shard_map(
        body,
        mesh=mesh,
        in_specs=(
            rows, P("fsdp"), cols, cols, cols, cols, P("fsdp"), cols, cols, cols,
            P(("fsdp", "replica"), None), rows,
        ),
        out_specs=(rows, rows, P("fsdp"), both, both, both, both, P("fsdp"), both, both, both),
        check_vma=False,
    )
```
